128 devices in a mesh: rows: 128 (over x, y, z, core).
Axes of the slice: x: 4, y: 4, z: 4, core: 2. Of those that a mesh axis runs over, the one named last changes fastest.
Arguments:
- points: float32 [49152, 256], P('rows'), may hold values from -6 to 6
- inv_scale: float32 [256], replicated, may hold values from 0.03 to 0.15
- noise: float32 [1], replicated, may hold values from 1 to 2
- prior: float32 [49152, 512], P('rows'), may hold values from -0.12 to 0.12
- active: int32 [3, 49152], P(None, 'rows'), may hold values from 0 to 1, as said below
- pivots: int32 [3, 128], replicated, may hold values from 0 to 49151, as said below
Outputs:
- new_factor: float32 [49152, 384], P('rows')
- residual_diag: float32 [49152], P('rows')
The draws below stay inside these ranges and needn't reach their ends.
Inputs may be any that keep to these rules, and one draw needn't show every extreme that they name: Rows active in panel p + 1 are active in panel p. In panel 0 exactly 96 times the number of devices rows are active in all; no device holds more than 336 active rows in a panel, and some device holds exactly 336 in panel 0. All 384 pivots are distinct, and a pivot of panel p is active in panels 0 to p.
All inputs are finite; a program needn't handle non-finite values.
Results may differ from the reference program's by a relative error of at most 0.0003.
Values sent between devices are 32-bit elements; how exact they have to be, the bound alone decides.
No kernel may reach another device: no remote copies, remote signals or barrier semaphores. Data moves between devices by JAX's collectives and lax.ppermute only.
A program may use at most 64 MiB of HBM per device.

```python
import math
import jax
import jax.numpy as jnp
from jax import lax

D = 256
R0 = 512
PANEL = 128
PANELS = 3
ROWS_DEV = 384
HELP_ROWS = 96
LIGHT = 16
POINTS = 49152
N_ROWS = 128


def layout_levels(key):
    base_key = jax.random.fold_in(key, 101)
    sub_keys = jax.random.split(base_key, 5)
    groups = N_ROWS // 4
    light_counts = jax.random.randint(sub_keys[0], (groups, 3), LIGHT, HELP_ROWS + 1)
    light_counts = light_counts.at[0].set(LIGHT)
    heavy_counts = 4 * HELP_ROWS - jnp.sum(light_counts, axis=1)
    grouped = jnp.concatenate([light_counts, heavy_counts[:, None]], axis=1).reshape(N_ROWS)
    device_order = jax.random.permutation(sub_keys[1], N_ROWS)
    counts = grouped[device_order]
    row_keys = jax.random.split(sub_keys[2], N_ROWS)
    ranking = jax.vmap(lambda row_key: jax.random.permutation(row_key, ROWS_DEV))(row_keys)
    thirds = counts // 3
    random_level = jax.random.randint(sub_keys[3], (N_ROWS, ROWS_DEV), 1, 4)
    levels = jnp.where(ranking < thirds[:, None], 3, jnp.where(ranking < counts[:, None], random_level, 0))
    return (levels.reshape(POINTS).astype(jnp.int32), sub_keys[4])


def draw_active(key, part):
    levels, unused = layout_levels(key)
    return jnp.stack([(levels > panel_index).astype(jnp.int32) for panel_index in range(PANELS)])


def draw_pivots(key, part):
    levels, pick_key = layout_levels(key)
    shuffle = jax.random.permutation(pick_key, POINTS).astype(jnp.int32)
    scores = (levels == 3).astype(jnp.int32) * 1048576 + shuffle
    chosen = lax.top_k(scores, PANELS * PANEL)[1]
    return chosen.reshape(PANELS, PANEL).astype(jnp.int32)


def draw_prior(key, part):
    sub_keys = jax.random.split(jax.random.fold_in(key, 202), 2)
    row_scale = jnp.exp(jax.random.uniform(sub_keys[0], (POINTS, 1), jnp.float32, math.log(0.3), math.log(3.0)))
    entries = jnp.clip(jax.random.normal(sub_keys[1], (POINTS, R0), jnp.float32), -4.0, 4.0)
    return (0.01 * row_scale * entries).astype(jnp.float32)


def block_levels(rng, dims, pieces, least, largest):
    level = 1.0
    for axis_at, parts in pieces:
        draws = jax.random.uniform(jax.random.fold_in(jax.random.fold_in(rng, 6), axis_at), (parts,), jnp.float32, least / len(pieces), largest / len(pieces))
        level = level * jnp.repeat(jnp.exp(draws), dims[axis_at] // parts).reshape((-1,) + (1,) * (len(dims) - 1 - axis_at))
    return level


def centred(key, extent, scale, bound, shards=(), kind=jnp.bfloat16):
    factor_of = block_levels(key, extent, shards, -0.22, 0.18) if shards else 1.0
    values = jax.random.normal(key, extent, jnp.float32) * scale * factor_of
    return jnp.minimum(jnp.maximum(values, -bound), bound).astype(kind)


def setup_inputs(seed: int = 0) -> dict:
    arg_keys = jax.random.split(jax.random.key(seed), 7)
    points = centred(arg_keys[0], (POINTS, D), 1.0, 6.0, ((0, 128),), jnp.float32)
    inv_scale = jnp.clip(jnp.exp(jax.random.uniform(arg_keys[1], (D,), jnp.float32, math.log(0.03), math.log(0.15))), 0.03, 0.15)
    noise = jnp.clip(jax.random.uniform(arg_keys[2], (1,), jnp.float32, 1.0, 2.0), 1.0, 2.0)
    prior = draw_prior(jax.random.fold_in(arg_keys[6], 71), 0)
    active = draw_active(jax.random.fold_in(arg_keys[6], 71), 0)
    pivots = draw_pivots(jax.random.fold_in(arg_keys[6], 71), 0)
    return {"points": points, "inv_scale": inv_scale, "noise": noise, "prior": prior, "active": active, "pivots": pivots}


def kernel_rows(left_points, left_squares, right_points, right_squares):
    inner = jnp.dot(left_points.astype(jnp.float32), right_points.T.astype(jnp.float32), precision=lax.Precision.HIGHEST, preferred_element_type=jnp.float32)
    return jnp.exp(-0.5 * (left_squares[:, None] + right_squares[None, :] - 2.0 * inner))

def reference(points, inv_scale, noise, prior, active, pivots):
    noise_level = noise[0]
    scaled = points * inv_scale[None, :]
    squares = jnp.sum(scaled * scaled, axis=1)
    row_ids = jnp.arange(POINTS, dtype=jnp.int32)
    factor_now = prior
    columns = []
    blocks = POINTS // ROWS_DEV
    for panel_index in range(PANELS):
        pivot_ids = pivots[panel_index]
        pivot_points = scaled[pivot_ids]
        pivot_squares = squares[pivot_ids]
        pivot_factor = factor_now[pivot_ids]
        block_matrix = kernel_rows(pivot_points, pivot_squares, pivot_points, pivot_squares)
        block_matrix = block_matrix + noise_level * jnp.eye(PANEL, dtype=jnp.float32)
        block_matrix = block_matrix - jnp.dot(pivot_factor.astype(jnp.float32), pivot_factor.T.astype(jnp.float32), precision=lax.Precision.HIGHEST, preferred_element_type=jnp.float32)
        lower_factor = jnp.linalg.cholesky(block_matrix)

        def solve_block(inputs):
            block_points, block_squares, block_factor, block_ids = inputs
            residual = kernel_rows(block_points, block_squares, pivot_points, pivot_squares)
            residual = residual + noise_level * (block_ids[:, None] == pivot_ids[None, :]).astype(jnp.float32)
            residual = residual - jnp.dot(block_factor.astype(jnp.float32), pivot_factor.T.astype(jnp.float32), precision=lax.Precision.HIGHEST, preferred_element_type=jnp.float32)
            return jax.scipy.linalg.solve_triangular(lower_factor, residual.T, lower=True).T
        solved = lax.map(solve_block, (scaled.reshape(blocks, ROWS_DEV, D), squares.reshape(blocks, ROWS_DEV), factor_now.reshape(blocks, ROWS_DEV, factor_now.shape[1]), row_ids.reshape(blocks, ROWS_DEV)))
        fresh = solved.reshape(POINTS, PANEL) * active[panel_index][:, None].astype(jnp.float32)
        columns.append(fresh)
        factor_now = jnp.concatenate([factor_now, fresh], axis=1)
    new_factor = jnp.concatenate(columns, axis=1)
    residual_diag = 1.0 + noise_level - jnp.sum(prior * prior, axis=1) - jnp.sum(new_factor * new_factor, axis=1)
    return (new_factor, residual_diag)
```

```python
import functools

import jax
import jax.numpy as jnp
from jax import lax
from jax.experimental import pallas as pl
from jax.experimental.pallas import tpu as pltpu
from jax.sharding import PartitionSpec as P

D = 256
R0 = 512
F = D + R0
PANEL = 128
PANELS = 3
PIV = PANEL * PANELS
HALF = PIV // 2
STRIP = 16
HI = lax.Precision.HIGHEST
BF = jnp.bfloat16
F32 = jnp.float32
NT = (((1,), (1,)), ((), ()))
NN = (((1,), (0,)), ((), ()))


def dot_hi(a, b, dims=NT):
    return lax.dot_general(a, b, dims, precision=HI, preferred_element_type=F32)


def split2(a):
    high = a.astype(BF)
    return high, (a - high.astype(F32)).astype(BF)


def split3(a):
    high, rest = a.astype(BF), None
    rest = a - high.astype(F32)
    mid = rest.astype(BF)
    return high, mid, (rest - mid.astype(F32)).astype(BF)


def dot_bf(a, b, dims=NT):
    return lax.dot_general(a, b, dims, preferred_element_type=F32)


def dot_x3(a, b, dims=NT):
    ah, al = split2(a)
    bh, bl = split2(b)
    return dot_bf(ah, bh, dims) + (dot_bf(ah, bl, dims) + dot_bf(al, bh, dims))


def column_of(row):
    return jnp.transpose(jnp.broadcast_to(row, (8, 128)))[:, 0:1]


def pack_kernel(place_ref, pivots_ref, points_ref, prior_ref, keep_ref, give_ref, all_ref):
    rows = points_ref.shape[0]
    core = place_ref[0]
    base = (place_ref[1] * rows).astype(F32)
    lanes = lax.broadcasted_iota(jnp.int32, (PANEL, rows), 1).astype(F32)
    parts = [split3(points_ref[...]), split3(prior_ref[...])]
    for panel in range(PANELS):
        wanted = column_of(pivots_ref[panel : panel + 1, :].astype(F32)) - base
        select = (lanes == wanted).astype(BF)
        at = 0
        for high, mid, low in parts:
            got = dot_bf(select, high, NN) + dot_bf(select, mid, NN)
            got = got + dot_bf(select, low, NN)
            all_ref[panel * PANEL : (panel + 1) * PANEL, at : at + got.shape[1]] = got
            at += got.shape[1]
    keep_ref[...] = all_ref[pl.ds(pl.multiple_of(core * HALF, HALF), HALF), :]
    give_ref[...] = all_ref[pl.ds(pl.multiple_of((1 - core) * HALF, HALF), HALF), :]


def fold_kernel(keep_ref, came_ref, out_ref):
    homes = out_ref.shape[0]
    for turn in range(HALF // homes):
        span = pl.ds(turn * homes, homes)
        out_ref[:, 0, turn * F : (turn + 1) * F] = keep_ref[span, :] + came_ref[span, :]


def factor(w_ref, z_ref, inv_ref):
    size = PANEL
    iota = lax.broadcasted_iota(jnp.int32, (STRIP, size), 0)
    wide = (STRIP, size)
    z_ref[...] = jnp.zeros_like(z_ref)
    for first in range(0, size, STRIP):
        left = w_ref[first : first + STRIP, 0:size]
        right = w_ref[first : first + STRIP, size : 2 * size]
        columns = [
            jnp.broadcast_to(left[:, first + j : first + j + 1], wide) for j in range(STRIP)
        ]
        for j in range(STRIP):
            root = lax.rsqrt(jnp.broadcast_to(columns[j][j : j + 1, :], wide))
            inverse = root * root
            row_left = jnp.broadcast_to(left[j : j + 1, :], wide)
            row_right = jnp.broadcast_to(right[j : j + 1, :], wide)
            inv_ref[first + j : first + j + 1, :] = row_right[0:1] * root[0:1]
            weight = jnp.where(iota == j, 1.0 - inverse, columns[j] * inverse)
            left = left - weight * row_left
            right = right - weight * row_right
            for m in range(j + 1, STRIP):
                columns[m] = columns[m] - weight * jnp.broadcast_to(columns[m][j : j + 1, :], wide)
        last = first + STRIP
        if last < size:
            z_ref[first:last, 0:size] = left
            z_ref[first:last, size : 2 * size] = right
            below = w_ref[last:size, 0:size]
            w_ref[last:size, :] = w_ref[last:size, :] - dot_hi(below, z_ref[...], NN)
            z_ref[first:last, :] = jnp.zeros((STRIP, 2 * size), F32)


def window_kernel(
    place_ref,
    noise_ref,
    pivots_ref,
    scale_ref,
    points_ref,
    prior_ref,
    active_ref,
    mine_ref,
    other_ref,
    new_ref,
    diag_ref,
    pp_ref,
    pf_ref,
    k_ref,
    w_ref,
    z_ref,
    inv_ref,
    x_ref,
):
    rows = points_ref.shape[0]
    homes = mine_ref.shape[0]
    core = place_ref[0]
    base = place_ref[1] * rows
    noise = noise_ref[0]
    scale = scale_ref[...]
    for turn in range(HALF // homes):
        for ref, half in ((mine_ref, core), (other_ref, 1 - core)):
            at = pl.ds(pl.multiple_of(half * HALF, HALF) + turn * homes, homes)
            pp_ref[at, :] = ref[:, 0, turn * F : turn * F + D] * scale
            pf_ref[at, :] = ref[:, 0, turn * F + D : (turn + 1) * F]
    ones = jnp.ones((8, D), F32)
    pp = pp_ref[...]
    pf = pf_ref[...]
    pp2 = pp * pp
    square_row = dot_hi(ones, pp2)[0:1, :]
    square_col = jnp.sum(pp2, axis=1, keepdims=True)
    mine = points_ref[...] * scale
    prior = prior_ref[...]
    mine_col = jnp.sum(mine * mine, axis=1, keepdims=True)
    eye = (
        lax.broadcasted_iota(jnp.int32, (PIV, PIV), 0)
        == lax.broadcasted_iota(jnp.int32, (PIV, PIV), 1)
    ).astype(F32)
    gram = jnp.exp(-0.5 * (square_col + square_row - 2.0 * dot_hi(pp, pp))) + noise * eye
    k_ref[...] = gram - dot_hi(pf, pf)
    residual = jnp.exp(-0.5 * (mine_col + square_row - 2.0 * dot_hi(mine, pp)))
    residual = residual - dot_hi(prior, pf)
    ids = base + lax.broadcasted_iota(jnp.int32, (rows, PANEL), 0)
    for panel in range(PANELS):
        span = slice(panel * PANEL, (panel + 1) * PANEL)
        same = (ids == pivots_ref[panel : panel + 1, :]).astype(F32)
        x_ref[:, span] = residual[:, span] + noise * same
    small_eye = eye[0:PANEL, 0:PANEL]
    total = dot_hi(jnp.ones((8, R0), F32), prior * prior)[0:1, :]
    for panel in range(PANELS):
        span = slice(panel * PANEL, (panel + 1) * PANEL)
        w_ref[:, 0:PANEL] = k_ref[span, span]
        w_ref[:, PANEL:] = small_eye
        factor(w_ref, z_ref, inv_ref)
        inverse = inv_ref[...]
        x_ref[:, span] = dot_hi(x_ref[:, span], inverse)
        if panel + 1 < PANELS:
            rest = slice((panel + 1) * PANEL, PIV)
            below = dot_hi(k_ref[rest, span], inverse)
            k_ref[rest, rest] = k_ref[rest, rest] - dot_hi(below, below)
            x_ref[:, rest] = x_ref[:, rest] - dot_hi(x_ref[:, span], below)
    for panel in range(PANELS):
        span = slice(panel * PANEL, (panel + 1) * PANEL)
        for block in range(rows // 128):
            here = slice(block * 128, (block + 1) * 128)
            mask = column_of(active_ref[panel : panel + 1, here].astype(F32))
            new_ref[here, span] = x_ref[here, span] * mask
    new = new_ref[...]
    total = total + dot_hi(jnp.ones((8, PIV), F32), new * new)[0:1, :]
    diag_ref[...] = 1.0 + noise - total


SMEM = pl.BlockSpec(memory_space=pltpu.SMEM)
VMEM = pl.BlockSpec(memory_space=pltpu.VMEM)


def local(points, inv_scale, noise, prior, active, pivots):
    rows = points.shape[0]
    devices = lax.axis_size("rows")
    homes = devices // 2
    index = lax.axis_index("rows")
    place = jnp.stack([index % 2, index]).astype(jnp.int32)
    partner = [(i, i ^ 1) for i in range(devices)]
    groups = [[2 * chip + core for chip in range(homes)] for core in range(2)]
    half = jax.ShapeDtypeStruct((HALF, F), F32)
    keep, give = pl.pallas_call(
        pack_kernel,
        out_shape=(half, half),
        in_specs=[SMEM, VMEM, VMEM, VMEM],
        out_specs=(VMEM, VMEM),
        scratch_shapes=[pltpu.VMEM((PIV, F), F32)],
        name="pack",
    )(place, pivots, points, prior)
    came = lax.ppermute(give, "rows", partner)
    wide = jax.ShapeDtypeStruct((homes, 1, HALF // homes * F), F32)
    spread = pl.pallas_call(
        fold_kernel, out_shape=wide, in_specs=[VMEM, VMEM], out_specs=VMEM, name="fold"
    )(keep, came)
    exchange = functools.partial(
        lax.all_to_all,
        axis_name="rows",
        split_axis=0,
        concat_axis=0,
        axis_index_groups=groups,
        tiled=True,
    )
    got = exchange(spread)
    owned = jnp.broadcast_to(jnp.sum(got, axis=0, keepdims=True), wide.shape)
    mine = exchange(owned)
    other = lax.ppermute(mine, "rows", partner)
    new, diag = pl.pallas_call(
        window_kernel,
        out_shape=(
            jax.ShapeDtypeStruct((rows, PIV), F32),
            jax.ShapeDtypeStruct((1, rows), F32),
        ),
        in_specs=[SMEM, SMEM] + [VMEM] * 7,
        out_specs=(VMEM, VMEM),
        scratch_shapes=[
            pltpu.VMEM((PIV, D), F32),
            pltpu.VMEM((PIV, R0), F32),
            pltpu.VMEM((PIV, PIV), F32),
            pltpu.VMEM((PANEL, 2 * PANEL), F32),
            pltpu.VMEM((PANEL, 2 * PANEL), F32),
            pltpu.VMEM((PANEL, PANEL), F32),
            pltpu.VMEM((rows, PIV), F32),
        ],
        name="window",
    )(place, noise, pivots, inv_scale.reshape(1, D), points, prior, active, mine, other)
    return (new, diag.reshape(rows))


def solution(mesh):
    return jax.shard_map(
        local,
        mesh=mesh,
        in_specs=(P("rows", None), P(), P(), P("rows", None), P(None, "rows"), P()),
        out_specs=(P("rows", None), P("rows")),
        check_vma=False,
    )
```

```python
import functools

import jax
import jax.numpy as jnp
from jax import lax
from jax.experimental import pallas as pl
from jax.experimental.pallas import tpu as pltpu
from jax.sharding import PartitionSpec as P

D = 256
R0 = 512
F = D + R0
PANEL = 128
PANELS = 3
PIV = PANEL * PANELS
HALF = PIV // 2
STRIP = 8
LOOK = 2
BF = jnp.bfloat16
F32 = jnp.float32
NT = (((1,), (1,)), ((), ()))
NN = (((1,), (0,)), ((), ()))


def split2(a):
    high = a.astype(BF)
    return high, (a - high.astype(F32)).astype(BF)


def split3(a):
    high = a.astype(BF)
    rest = a - high.astype(F32)
    mid = rest.astype(BF)
    return high, mid, (rest - mid.astype(F32)).astype(BF)


def dot_bf(a, b, dims=NT):
    return lax.dot_general(a, b, dims, preferred_element_type=F32)


def dot_x3(a, b, dims=NT):
    return three(split2(a), split2(b), dims)


def three(a, b, dims=NT):
    return dot_bf(a[0], b[0], dims) + (dot_bf(a[0], b[1], dims) + dot_bf(a[1], b[0], dims))


def six(a, b, dims=NT):
    small = dot_bf(a[0], b[2], dims) + dot_bf(a[1], b[1], dims) + dot_bf(a[2], b[0], dims)
    return dot_bf(a[0], b[0], dims) + (dot_bf(a[0], b[1], dims) + dot_bf(a[1], b[0], dims) + small)


def column_of(row):
    return jnp.transpose(jnp.broadcast_to(row, (8, 128)))[:, 0:1]


def pack_kernel(pivots_ref, points_ref, prior_ref, keep_ref, give_ref, all_ref):
    rows = points_ref.shape[0]
    index = lax.axis_index("rows")
    core = lax.rem(index, 2)
    base = (index * rows).astype(F32)
    lanes = lax.broadcasted_iota(jnp.int32, (PANEL, rows), 1).astype(F32)
    parts = [split3(points_ref[...]), split3(prior_ref[...])]
    for panel in range(PANELS):
        wanted = column_of(pivots_ref[panel : panel + 1, :].astype(F32)) - base
        select = (lanes == wanted).astype(BF)
        at = 0
        for high, mid, low in parts:
            got = dot_bf(select, high, NN) + dot_bf(select, mid, NN)
            got = got + dot_bf(select, low, NN)
            all_ref[panel * PANEL : (panel + 1) * PANEL, at : at + got.shape[1]] = got
            at += got.shape[1]
    keep_ref[...] = all_ref[pl.ds(pl.multiple_of(core * HALF, HALF), HALF), :]
    give_ref[...] = all_ref[pl.ds(pl.multiple_of((1 - core) * HALF, HALF), HALF), :]


def fold_kernel(keep_ref, came_ref, out_ref):
    homes = out_ref.shape[0]
    for turn in range(HALF // homes):
        span = pl.ds(turn * homes, homes)
        out_ref[:, 0, turn * F : (turn + 1) * F] = keep_ref[span, :] + came_ref[span, :]


def spread_lane(block, lane):
    return jnp.broadcast_to(block[:, lane : lane + 1], (STRIP, PANEL))


def spread_row(block, row):
    return jnp.broadcast_to(block[row : row + 1, :], (STRIP, PANEL))


def factor(w_ref, z_ref, inv_ref):
    size = PANEL
    strips = size // STRIP
    iota = lax.broadcasted_iota(jnp.int32, (STRIP, size), 0)
    z_ref[...] = jnp.zeros_like(z_ref)
    left, right, ready = {}, {}, {}
    for strip in range(strips):
        first = STRIP * strip
        after = first + STRIP
        groups = range(min(LOOK + 1, strips - strip))
        for group in groups:
            if strip + group not in left:
                rows = slice(first + STRIP * group, after + STRIP * group)
                left[strip + group] = w_ref[rows, 0:size]
                right[strip + group] = w_ref[rows, size : 2 * size]
        column = {}
        for group in groups:
            for j in range(STRIP):
                if group == 0 and strip > 0:
                    column[group, j] = ready[j]
                else:
                    column[group, j] = spread_lane(left[strip + group], first + j)
        ready = {}
        if strip + 1 < strips:
            ready = {m: spread_lane(left[strip + 1], after + m) for m in range(STRIP)}
        for j in range(STRIP):
            root = lax.rsqrt(spread_row(column[0, j], j))
            inverse = root * root
            row_left = spread_row(left[strip], j)
            row_right = spread_row(right[strip], j)
            inv_ref[first + j : first + j + 1, :] = row_right[0:1] * root[0:1]
            own = {m: spread_row(column[0, m], j) for m in range(j + 1, STRIP)}
            ahead = {m: spread_row(column[1, j], m) for m in ready}
            for group in groups:
                weight = column[group, j] * inverse
                if group == 0:
                    weight = jnp.where(iota == j, 1.0 - inverse, weight)
                for m in own:
                    column[group, m] = column[group, m] - weight * own[m]
                if group == 1:
                    for m in ready:
                        ready[m] = ready[m] - weight * ahead[m]
                left[strip + group] = left[strip + group] - weight * row_left
                right[strip + group] = right[strip + group] - weight * row_right
        last = first + STRIP * (LOOK + 1)
        if last < size:
            if strip > 0:
                z_ref[first - STRIP : first, :] = jnp.zeros((STRIP, 2 * size), F32)
            z_ref[first:after, 0:size] = left[strip]
            z_ref[first:after, size : 2 * size] = right[strip]
            update = dot_x3(w_ref[last:size, 0:size], z_ref[...], NN)
            w_ref[last:size, :] = w_ref[last:size, :] - update


def row_of(column):
    return jnp.transpose(jnp.broadcast_to(column, (PANEL, PANEL)))[0:1, :]


def window_kernel(
    noise_ref,
    pivots_ref,
    scale_ref,
    active_ref,
    mine_hbm,
    other_hbm,
    points_hbm,
    prior_hbm,
    new_hbm,
    diag_ref,
    mine_ref,
    other_ref,
    points_ref,
    prior_ref,
    pp_ref,
    pf_ref,
    k_ref,
    w_ref,
    z_ref,
    inv_ref,
    x_ref,
    sems,
    out_sems,
):
    loads = [
        pltpu.make_async_copy(source, target, sems.at[i])
        for i, (source, target) in enumerate(
            (
                (mine_hbm, mine_ref),
                (other_hbm, other_ref),
                (points_hbm, points_ref),
                (prior_hbm, prior_ref),
            )
        )
    ]
    for load in loads:
        load.start()
    rows = points_ref.shape[0]
    homes = mine_ref.shape[0]
    index = lax.axis_index("rows")
    core = lax.rem(index, 2)
    base = index * rows
    noise = noise_ref[0]
    scale = scale_ref[...]
    for load, ref, half in ((loads[0], mine_ref, core), (loads[1], other_ref, 1 - core)):
        load.wait()
        for turn in range(HALF // homes):
            at = pl.ds(pl.multiple_of(half * HALF, HALF) + turn * homes, homes)
            pp_ref[at, :] = ref[:, 0, turn * F : turn * F + D] * scale
            pf_ref[at, :] = ref[:, 0, turn * F + D : (turn + 1) * F]
    pp = pp_ref[...]
    pp3 = split3(pp)
    pf2 = split2(pf_ref[...])
    square_col = jnp.sum(pp * pp, axis=1, keepdims=True)
    square_row = jnp.concatenate(
        [row_of(square_col[i * PANEL : (i + 1) * PANEL]) for i in range(PANELS)], axis=1
    )
    eye = (
        lax.broadcasted_iota(jnp.int32, (PIV, PIV), 0)
        == lax.broadcasted_iota(jnp.int32, (PIV, PIV), 1)
    ).astype(F32)
    gram = jnp.exp(-0.5 * (square_col + square_row - 2.0 * six(pp3, pp3))) + noise * eye
    k_ref[...] = gram - three(pf2, pf2)
    loads[2].wait()
    loads[3].wait()
    mine = points_ref[...] * scale
    prior = prior_ref[...]
    mine_col = jnp.sum(mine * mine, axis=1, keepdims=True)
    residual = jnp.exp(-0.5 * (mine_col + square_row - 2.0 * six(split3(mine), pp3)))
    residual = residual - three(split2(prior), pf2)
    ids = base + lax.broadcasted_iota(jnp.int32, (rows, PANEL), 0)
    for panel in range(PANELS):
        span = slice(panel * PANEL, (panel + 1) * PANEL)
        same = (ids == pivots_ref[panel : panel + 1, :]).astype(F32)
        x_ref[:, span] = residual[:, span] + noise * same
    small_eye = eye[0:PANEL, 0:PANEL]
    total = jnp.sum(prior * prior, axis=1, keepdims=True)
    stores = []
    for panel in range(PANELS):
        span = slice(panel * PANEL, (panel + 1) * PANEL)
        w_ref[:, 0:PANEL] = k_ref[span, span]
        w_ref[:, PANEL:] = small_eye
        factor(w_ref, z_ref, inv_ref)
        inverse = split2(inv_ref[...])
        if panel + 1 < PANELS:
            rest = slice((panel + 1) * PANEL, PIV)
            below = split2(three(split2(k_ref[rest, span]), inverse))
            k_ref[rest, rest] = k_ref[rest, rest] - three(below, below)
        fresh = three(split2(x_ref[:, span]), inverse)
        mask = jnp.concatenate(
            [
                column_of(active_ref[panel : panel + 1, i * 128 : (i + 1) * 128].astype(F32))
                for i in range(rows // 128)
            ],
            axis=0,
        )
        fresh = fresh * mask
        x_ref[:, span] = fresh
        store = pltpu.make_async_copy(x_ref.at[:, span], new_hbm.at[:, span], out_sems.at[panel])
        store.start()
        stores.append(store)
        total = total + jnp.sum(fresh * fresh, axis=1, keepdims=True)
        if panel + 1 < PANELS:
            x_ref[:, rest] = x_ref[:, rest] - three(split2(fresh), below)
    diag = (1.0 + noise) - total
    for i in range(rows // 128):
        diag_ref[:, i * 128 : (i + 1) * 128] = row_of(diag[i * 128 : (i + 1) * 128])
    for store in stores:
        store.wait()


SMEM = pl.BlockSpec(memory_space=pltpu.SMEM)
VMEM = pl.BlockSpec(memory_space=pltpu.VMEM)
ANY = pl.BlockSpec(memory_space=pl.ANY)


def local(points, inv_scale, noise, prior, active, pivots):
    rows = points.shape[0]
    devices = lax.axis_size("rows")
    homes = devices // 2
    partner = [(i, i ^ 1) for i in range(devices)]
    groups = [[2 * chip + core for chip in range(homes)] for core in range(2)]
    half = jax.ShapeDtypeStruct((HALF, F), F32)
    keep, give = pl.pallas_call(
        pack_kernel,
        out_shape=(half, half),
        in_specs=[VMEM, VMEM, VMEM],
        out_specs=(VMEM, VMEM),
        scratch_shapes=[pltpu.VMEM((PIV, F), F32)],
        name="pack",
    )(pivots, points, prior)
    came = lax.ppermute(give, "rows", partner)
    wide = jax.ShapeDtypeStruct((homes, 1, HALF // homes * F), F32)
    spread = pl.pallas_call(
        fold_kernel, out_shape=wide, in_specs=[VMEM, VMEM], out_specs=VMEM, name="fold"
    )(keep, came)
    exchange = functools.partial(
        lax.all_to_all,
        axis_name="rows",
        split_axis=0,
        concat_axis=0,
        axis_index_groups=groups,
        tiled=True,
    )
    got = exchange(spread)
    owned = jnp.broadcast_to(jnp.sum(got, axis=0, keepdims=True), wide.shape)
    mine = exchange(owned)
    other = lax.ppermute(mine, "rows", partner)
    new, diag = pl.pallas_call(
        window_kernel,
        out_shape=(
            jax.ShapeDtypeStruct((rows, PIV), F32),
            jax.ShapeDtypeStruct((1, rows), F32),
        ),
        in_specs=[SMEM, VMEM, VMEM, VMEM] + [ANY] * 4,
        out_specs=(ANY, VMEM),
        scratch_shapes=[
            pltpu.VMEM(wide.shape, F32),
            pltpu.VMEM(wide.shape, F32),
            pltpu.VMEM((rows, D), F32),
            pltpu.VMEM((rows, R0), F32),
            pltpu.VMEM((PIV, D), F32),
            pltpu.VMEM((PIV, R0), F32),
            pltpu.VMEM((PIV, PIV), F32),
            pltpu.VMEM((PANEL, 2 * PANEL), F32),
            pltpu.VMEM((PANEL, 2 * PANEL), F32),
            pltpu.VMEM((PANEL, PANEL), F32),
            pltpu.VMEM((rows, PIV), F32),
            pltpu.SemaphoreType.DMA((4,)),
            pltpu.SemaphoreType.DMA((PANELS,)),
        ],
        name="window",
    )(noise, pivots, inv_scale.reshape(1, D), active, mine, other, points, prior)
    return (new, diag.reshape(rows))


def solution(mesh):
    return jax.shard_map(
        local,
        mesh=mesh,
        in_specs=(P("rows", None), P(), P(), P("rows", None), P(None, "rows"), P()),
        out_specs=(P("rows", None), P("rows")),
        check_vma=False,
    )
```

```python
import functools

import jax
import jax.numpy as jnp
from jax import lax
from jax.experimental import pallas as pl
from jax.experimental.pallas import tpu as pltpu
from jax.sharding import PartitionSpec as P

D = 256
R0 = 512
F = D + R0
PANEL = 128
PANELS = 3
PIV = PANEL * PANELS
HALF = PIV // 2
STRIP = 8
LOOK = 2
BF = jnp.bfloat16
F32 = jnp.float32
NT = (((1,), (1,)), ((), ()))
NN = (((1,), (0,)), ((), ()))


def split2(a):
    high = a.astype(BF)
    return high, (a - high.astype(F32)).astype(BF)


def split3(a):
    high = a.astype(BF)
    rest = a - high.astype(F32)
    mid = rest.astype(BF)
    return high, mid, (rest - mid.astype(F32)).astype(BF)


def dot_bf(a, b, dims=NT):
    return lax.dot_general(a, b, dims, preferred_element_type=F32)


def dot_x3(a, b, dims=NT):
    return three(split2(a), split2(b), dims)


def three(a, b, dims=NT):
    return dot_bf(a[0], b[0], dims) + (dot_bf(a[0], b[1], dims) + dot_bf(a[1], b[0], dims))


def six(a, b, dims=NT):
    small = dot_bf(a[0], b[2], dims) + dot_bf(a[1], b[1], dims) + dot_bf(a[2], b[0], dims)
    return dot_bf(a[0], b[0], dims) + (dot_bf(a[0], b[1], dims) + dot_bf(a[1], b[0], dims) + small)


def column_of(row):
    return jnp.transpose(jnp.broadcast_to(row, (8, 128)))[:, 0:1]


def pivot_columns(pivots_ref):
    return [column_of(pivots_ref[p : p + 1, :].astype(F32)) for p in range(PANELS)]


def pivot_order(pivots_ref):
    smaller = []
    for column in pivot_columns(pivots_ref):
        ahead = [
            (pivots_ref[p : p + 1, :].astype(F32) < column).astype(F32) for p in range(PANELS)
        ]
        smaller.append(jnp.sum(ahead[0] + ahead[1] + ahead[2], axis=1, keepdims=True))
    return jnp.concatenate(smaller, axis=0)


def count_rows(tests):
    total = tests[0].astype(F32)
    for test in tests[1:]:
        total = total + test.astype(F32)
    return jnp.sum(total, axis=0, keepdims=True)


def pack_kernel(turn_ref, pivots_ref, points_ref, prior_ref, send_ref, pick_ref, turns_ref):
    rows = points_ref.shape[0]
    devices = send_ref.shape[0]
    index = lax.axis_index("rows")
    turn = turn_ref[0].astype(F32)
    base = (index * rows).astype(F32)
    columns = pivot_columns(pivots_ref)
    ids = base + lax.broadcasted_iota(jnp.int32, (1, rows), 1).astype(F32)
    place = count_rows([column < ids for column in columns])
    found = count_rows([column == ids for column in columns])
    step = place - place[:, 0:1] - devices * turn
    home = place - devices * jnp.floor(place * (1.0 / devices))
    home = jnp.where((found > 0.5) & (step >= 0.0) & (step < devices), home, -1.0)
    target = lax.broadcasted_iota(jnp.int32, (devices, rows), 0).astype(F32)
    select = (target == home).astype(BF)
    at = 0
    for ref in (points_ref, prior_ref):
        high, mid, low = split3(ref[...])
        got = dot_bf(select, high, NN) + dot_bf(select, mid, NN) + dot_bf(select, low, NN)
        send_ref[:, 0, at : at + got.shape[1]] = got
        at += got.shape[1]
    edges = rows * lax.broadcasted_iota(jnp.int32, (1, devices), 1).astype(F32)
    start = count_rows([column < edges for column in columns])
    stop = count_rows([column < edges + rows for column in columns])
    slot = lax.broadcasted_iota(jnp.int32, (8, devices), 0)
    wanted = index.astype(F32) + devices * slot.astype(F32)
    step = wanted - start - devices * turn
    pick = (wanted >= start) & (wanted < stop) & (step >= 0.0) & (step < devices)
    pick_ref[...] = (pick & (slot < PIV // devices)).astype(F32)
    longest = jnp.max(stop - start)
    turns_ref[0] = jnp.where(longest > 2 * devices, 3, jnp.where(longest > devices, 2, 1))


def pick_kernel(pick_ref, came_ref, out_ref, rows_ref):
    rows_ref[...] = came_ref[:, 0, :]
    select = pick_ref[...].astype(BF)
    high, mid, low = split3(rows_ref[...])
    got = dot_bf(select, high, NN) + dot_bf(select, mid, NN) + dot_bf(select, low, NN)
    for row in range(out_ref.shape[2] // F):
        out_ref[0, :, row * F : (row + 1) * F] = got[row : row + 1, :]


def spread_lane(block, lane):
    return jnp.broadcast_to(block[:, lane : lane + 1], (STRIP, PANEL))


def spread_row(block, row):
    return jnp.broadcast_to(block[row : row + 1, :], (STRIP, PANEL))


def factor(w_ref, z_ref, inv_ref):
    size = PANEL
    strips = size // STRIP
    iota = lax.broadcasted_iota(jnp.int32, (STRIP, size), 0)
    z_ref[...] = jnp.zeros_like(z_ref)
    left, right, ready = {}, {}, {}
    for strip in range(strips):
        first = STRIP * strip
        after = first + STRIP
        groups = range(min(LOOK + 1, strips - strip))
        for group in groups:
            if strip + group not in left:
                rows = slice(first + STRIP * group, after + STRIP * group)
                left[strip + group] = w_ref[rows, 0:size]
                right[strip + group] = w_ref[rows, size : 2 * size]
        column = {}
        for group in groups:
            for j in range(STRIP):
                if group == 0 and strip > 0:
                    column[group, j] = ready[j]
                else:
                    column[group, j] = spread_lane(left[strip + group], first + j)
        ready = {}
        if strip + 1 < strips:
            ready = {m: spread_lane(left[strip + 1], after + m) for m in range(STRIP)}
        for j in range(STRIP):
            root = lax.rsqrt(spread_row(column[0, j], j))
            inverse = root * root
            row_left = spread_row(left[strip], j)
            row_right = spread_row(right[strip], j)
            inv_ref[first + j : first + j + 1, :] = row_right[0:1] * root[0:1]
            own = {m: spread_row(column[0, m], j) for m in range(j + 1, STRIP)}
            ahead = {m: spread_row(column[1, j], m) for m in ready}
            for group in groups:
                weight = column[group, j] * inverse
                if group == 0:
                    weight = jnp.where(iota == j, 1.0 - inverse, weight)
                for m in own:
                    column[group, m] = column[group, m] - weight * own[m]
                if group == 1:
                    for m in ready:
                        ready[m] = ready[m] - weight * ahead[m]
                left[strip + group] = left[strip + group] - weight * row_left
                right[strip + group] = right[strip + group] - weight * row_right
        last = first + STRIP * (LOOK + 1)
        if last < size:
            if strip > 0:
                z_ref[first - STRIP : first, :] = jnp.zeros((STRIP, 2 * size), F32)
            z_ref[first:after, 0:size] = left[strip]
            z_ref[first:after, size : 2 * size] = right[strip]
            update = dot_x3(w_ref[last:size, 0:size], z_ref[...], NN)
            w_ref[last:size, :] = w_ref[last:size, :] - update


def row_of(column):
    return jnp.transpose(jnp.broadcast_to(column, (PANEL, PANEL)))[0:1, :]


def window_kernel(
    noise_ref,
    pivots_ref,
    scale_ref,
    active_ref,
    mine_ref,
    other_ref,
    points_ref,
    prior_ref,
    new_hbm,
    diag_ref,
    g_ref,
    k_ref,
    w_ref,
    z_ref,
    inv_ref,
    x_ref,
    out_sems,
):
    rows = points_ref.shape[0]
    homes = mine_ref.shape[0]
    index = lax.axis_index("rows")
    core = lax.rem(index, 2)
    base = index * rows
    noise = noise_ref[0]
    scale = scale_ref[...]
    for ref, half in ((mine_ref, core), (other_ref, 1 - core)):
        for turn in range(HALF // homes):
            at = pl.ds(pl.multiple_of(half * HALF, HALF) + turn * homes, homes)
            g_ref[at, :] = ref[:, 0, turn * F : (turn + 1) * F]
    order = pivot_order(pivots_ref)
    lane = lax.broadcasted_iota(jnp.int32, (1, PIV), 1)
    half, turn, home = lane // HALF, lane % HALF // homes, lane % homes
    held = (2 * home + half + 2 * homes * turn).astype(F32)
    place = (order == held).astype(BF)
    pp3 = [dot_bf(place, part, NN) for part in split3(g_ref[:, 0:D] * scale)]
    pp = pp3[0] + pp3[1] + pp3[2]
    pp3 = [part.astype(BF) for part in pp3]
    pf2 = [dot_bf(place, part, NN).astype(BF) for part in split2(g_ref[:, D:F])]
    square_col = jnp.sum(pp * pp, axis=1, keepdims=True)
    square_row = jnp.concatenate(
        [row_of(square_col[i * PANEL : (i + 1) * PANEL]) for i in range(PANELS)], axis=1
    )
    eye = (
        lax.broadcasted_iota(jnp.int32, (PIV, PIV), 0)
        == lax.broadcasted_iota(jnp.int32, (PIV, PIV), 1)
    ).astype(F32)
    gram = jnp.exp(-0.5 * (square_col + square_row - 2.0 * six(pp3, pp3))) + noise * eye
    k_ref[...] = gram - three(pf2, pf2)
    mine = points_ref[...] * scale
    prior = prior_ref[...]
    mine_col = jnp.sum(mine * mine, axis=1, keepdims=True)
    residual = jnp.exp(-0.5 * (mine_col + square_row - 2.0 * six(split3(mine), pp3)))
    residual = residual - three(split2(prior), pf2)
    ids = base + lax.broadcasted_iota(jnp.int32, (rows, PANEL), 0)
    for panel in range(PANELS):
        span = slice(panel * PANEL, (panel + 1) * PANEL)
        same = (ids == pivots_ref[panel : panel + 1, :]).astype(F32)
        x_ref[:, span] = residual[:, span] + noise * same
    small_eye = eye[0:PANEL, 0:PANEL]
    total = jnp.sum(prior * prior, axis=1, keepdims=True)
    stores = []
    for panel in range(PANELS):
        span = slice(panel * PANEL, (panel + 1) * PANEL)
        w_ref[:, 0:PANEL] = k_ref[span, span]
        w_ref[:, PANEL:] = small_eye
        factor(w_ref, z_ref, inv_ref)
        inverse = split2(inv_ref[...])
        if panel + 1 < PANELS:
            rest = slice((panel + 1) * PANEL, PIV)
            below = split2(three(split2(k_ref[rest, span]), inverse))
            k_ref[rest, rest] = k_ref[rest, rest] - three(below, below)
        fresh = three(split2(x_ref[:, span]), inverse)
        mask = jnp.concatenate(
            [
                column_of(active_ref[panel : panel + 1, i * 128 : (i + 1) * 128].astype(F32))
                for i in range(rows // 128)
            ],
            axis=0,
        )
        fresh = fresh * mask
        x_ref[:, span] = fresh
        store = pltpu.make_async_copy(x_ref.at[:, span], new_hbm.at[:, span], out_sems.at[panel])
        store.start()
        stores.append(store)
        total = total + jnp.sum(fresh * fresh, axis=1, keepdims=True)
        if panel + 1 < PANELS:
            x_ref[:, rest] = x_ref[:, rest] - three(split2(fresh), below)
    diag = (1.0 + noise) - total
    for i in range(rows // 128):
        diag_ref[i * 128 : (i + 1) * 128] = row_of(diag[i * 128 : (i + 1) * 128])[0]
    for store in stores:
        store.wait()


SMEM = pl.BlockSpec(memory_space=pltpu.SMEM)
VMEM = pl.BlockSpec(memory_space=pltpu.VMEM)
SMALL = pltpu.CompilerParams(vmem_limit_bytes=16 * 1024 * 1024)
ANY = pl.BlockSpec(memory_space=pl.ANY)


def local(points, inv_scale, noise, prior, active, pivots):
    rows = points.shape[0]
    devices = lax.axis_size("rows")
    homes = devices // 2
    partner = [(i, i ^ 1) for i in range(devices)]
    groups = [[2 * chip + core for chip in range(homes)] for core in range(2)]
    exchange = functools.partial(
        lax.all_to_all, axis_name="rows", split_axis=0, concat_axis=0, tiled=True
    )
    def routed(turn):
        send, pick, turns = pl.pallas_call(
            pack_kernel,
            out_shape=(
                jax.ShapeDtypeStruct((devices, 1, F), F32),
                jax.ShapeDtypeStruct((8, devices), F32),
                jax.ShapeDtypeStruct((1,), jnp.int32),
            ),
            in_specs=[SMEM, VMEM, VMEM, VMEM],
            out_specs=(VMEM, VMEM, SMEM),
            name="pack",
            compiler_params=SMALL,
        )(turn, pivots, points, prior)
        owned = pl.pallas_call(
            pick_kernel,
            out_shape=jax.ShapeDtypeStruct((1, 1, PIV // devices * F), F32),
            in_specs=[VMEM, VMEM],
            out_specs=VMEM,
            scratch_shapes=[pltpu.VMEM((devices, F), F32)],
            name="pick",
            compiler_params=SMALL,
        )(pick, exchange(send))
        return owned, turns[0]

    owned, turns = routed(jnp.zeros((1,), jnp.int32))

    def more(state):
        return state[0] < turns

    def again(state):
        turn, owned = state
        return turn + 1, owned + routed(turn[None])[0]

    owned = lax.while_loop(more, again, (jnp.int32(1), owned))[1]
    mine = exchange(jnp.broadcast_to(owned, (homes, *owned.shape[1:])), axis_index_groups=groups)
    other = lax.ppermute(mine, "rows", partner)
    return pl.pallas_call(
        window_kernel,
        out_shape=(
            jax.ShapeDtypeStruct((rows, PIV), F32),
            jax.ShapeDtypeStruct((rows,), F32),
        ),
        in_specs=[SMEM] + [VMEM] * 7,
        out_specs=(ANY, VMEM),
        scratch_shapes=[
            pltpu.VMEM((PIV, F), F32),
            pltpu.VMEM((PIV, PIV), F32),
            pltpu.VMEM((PANEL, 2 * PANEL), F32),
            pltpu.VMEM((PANEL, 2 * PANEL), F32),
            pltpu.VMEM((PANEL, PANEL), F32),
            pltpu.VMEM((rows, PIV), F32),
            pltpu.SemaphoreType.DMA((PANELS,)),
        ],
        name="window",
        compiler_params=SMALL,
    )(noise, pivots, inv_scale.reshape(1, D), active, mine, other, points, prior)


def solution(mesh):
    return jax.shard_map(
        local,
        mesh=mesh,
        in_specs=(P("rows", None), P(), P(), P("rows", None), P(None, "rows"), P()),
        out_specs=(P("rows", None), P("rows")),
        check_vma=False,
    )
```

```python
import functools

import jax
import jax.numpy as jnp
from jax import lax
from jax.experimental import pallas as pl
from jax.experimental.pallas import tpu as pltpu
from jax.sharding import PartitionSpec as P

D = 256
R0 = 512
F = D + R0
PANEL = 128
PANELS = 3
PIV = PANEL * PANELS
HALF = PIV // 2
STRIP = 8
LOOK = 2
BF = jnp.bfloat16
F32 = jnp.float32
NT = (((1,), (1,)), ((), ()))
NN = (((1,), (0,)), ((), ()))


def split2(a):
    high = a.astype(BF)
    return high, (a - high.astype(F32)).astype(BF)


def split3(a):
    high = a.astype(BF)
    rest = a - high.astype(F32)
    mid = rest.astype(BF)
    return high, mid, (rest - mid.astype(F32)).astype(BF)


def dot_bf(a, b, dims=NT):
    return lax.dot_general(a, b, dims, preferred_element_type=F32)


def dot_x3(a, b, dims=NT):
    return three(split2(a), split2(b), dims)


def three(a, b, dims=NT):
    return dot_bf(a[0], b[0], dims) + (dot_bf(a[0], b[1], dims) + dot_bf(a[1], b[0], dims))


def column_of(row):
    return jnp.transpose(jnp.broadcast_to(row, (8, 128)))[:, 0:1]


def pivot_columns(pivots_ref):
    return [column_of(pivots_ref[p : p + 1, :].astype(F32)) for p in range(PANELS)]


def pivot_order(pivots_ref):
    smaller = []
    for column in pivot_columns(pivots_ref):
        ahead = [
            (pivots_ref[p : p + 1, :].astype(F32) < column).astype(F32) for p in range(PANELS)
        ]
        smaller.append(jnp.sum(ahead[0] + ahead[1] + ahead[2], axis=1, keepdims=True))
    return jnp.concatenate(smaller, axis=0)


def count_rows(tests):
    total = tests[0].astype(F32)
    for test in tests[1:]:
        total = total + test.astype(F32)
    return jnp.sum(total, axis=0, keepdims=True)


def pack_kernel(
    turn_ref,
    pivots_ref,
    points_hbm,
    prior_hbm,
    send_ref,
    pick_ref,
    turns_ref,
    kept_ref,
    points_ref,
    prior_ref,
    sems,
):
    loads = [
        pltpu.make_async_copy(source, target, sems.at[i])
        for i, (source, target) in enumerate(
            ((points_hbm, points_ref), (prior_hbm, prior_ref))
        )
    ]
    for load in loads:
        load.start()
    rows = points_ref.shape[0]
    devices = send_ref.shape[0]
    index = lax.axis_index("rows")
    turn = turn_ref[0].astype(F32)
    base = (index * rows).astype(F32)
    kept_ref[...] = pivots_ref[...]
    columns = pivot_columns(pivots_ref)
    ids = base + lax.broadcasted_iota(jnp.int32, (1, rows), 1).astype(F32)
    place = count_rows([column < ids for column in columns])
    found = count_rows([column == ids for column in columns])
    step = place - place[:, 0:1] - devices * turn
    home = place - devices * jnp.floor(place * (1.0 / devices))
    home = jnp.where((found > 0.5) & (step >= 0.0) & (step < devices), home, -1.0)
    target = lax.broadcasted_iota(jnp.int32, (devices, rows), 0).astype(F32)
    select = (target == home).astype(BF)
    edges = rows * lax.broadcasted_iota(jnp.int32, (1, devices), 1).astype(F32)
    start = count_rows([column < edges for column in columns])
    stop = count_rows([column < edges + rows for column in columns])
    slot = lax.broadcasted_iota(jnp.int32, (8, devices), 0)
    wanted = index.astype(F32) + devices * slot.astype(F32)
    step = wanted - start - devices * turn
    pick = (wanted >= start) & (wanted < stop) & (step >= 0.0) & (step < devices)
    pick_ref[...] = (pick & (slot < PIV // devices)).astype(F32)
    longest = jnp.max(stop - start)
    turns_ref[0] = jnp.where(longest > 2 * devices, 3, jnp.where(longest > devices, 2, 1))
    at = 0
    for load, ref in ((loads[0], points_ref), (loads[1], prior_ref)):
        load.wait()
        high, mid, low = split3(ref[...])
        got = dot_bf(select, high, NN) + dot_bf(select, mid, NN) + dot_bf(select, low, NN)
        send_ref[:, 0, at : at + got.shape[1]] = got
        at += got.shape[1]


def pick_kernel(pick_ref, came_ref, out_ref, rows_ref):
    rows_ref[...] = came_ref[:, 0, :]
    select = pick_ref[...].astype(BF)
    high, mid, low = split3(rows_ref[...])
    got = dot_bf(select, high, NN) + dot_bf(select, mid, NN) + dot_bf(select, low, NN)
    for row in range(out_ref.shape[2] // F):
        out_ref[0, :, row * F : (row + 1) * F] = got[row : row + 1, :]


def spread_lane(block, lane):
    return jnp.broadcast_to(block[:, lane : lane + 1], (STRIP, PANEL))


def spread_row(block, row):
    return jnp.broadcast_to(block[row : row + 1, :], (STRIP, PANEL))


def factor(w_ref, z_ref, inv_ref):
    size = PANEL
    strips = size // STRIP
    iota = lax.broadcasted_iota(jnp.int32, (STRIP, size), 0)
    z_ref[...] = jnp.zeros_like(z_ref)
    left, right, ready = {}, {}, {}
    for strip in range(strips):
        first = STRIP * strip
        after = first + STRIP
        groups = range(min(LOOK + 1, strips - strip))
        for group in groups:
            if strip + group not in left:
                rows = slice(first + STRIP * group, after + STRIP * group)
                left[strip + group] = w_ref[rows, 0:size]
                right[strip + group] = w_ref[rows, size : 2 * size]
        column = {}
        for group in groups:
            for j in range(STRIP):
                if group == 0 and strip > 0:
                    column[group, j] = ready[j]
                else:
                    column[group, j] = spread_lane(left[strip + group], first + j)
        ready = {}
        if strip + 1 < strips:
            ready = {m: spread_lane(left[strip + 1], after + m) for m in range(STRIP)}
        for j in range(STRIP):
            root = lax.rsqrt(spread_row(column[0, j], j))
            inverse = root * root
            row_left = spread_row(left[strip], j)
            row_right = spread_row(right[strip], j)
            inv_ref[first + j : first + j + 1, :] = row_right[0:1] * root[0:1]
            own = {m: spread_row(column[0, m], j) for m in range(j + 1, STRIP)}
            ahead = {m: spread_row(column[1, j], m) for m in ready}
            for group in groups:
                weight = column[group, j] * inverse
                if group == 0:
                    weight = jnp.where(iota == j, 1.0 - inverse, weight)
                for m in own:
                    column[group, m] = column[group, m] - weight * own[m]
                if group == 1:
                    for m in ready:
                        ready[m] = ready[m] - weight * ahead[m]
                left[strip + group] = left[strip + group] - weight * row_left
                right[strip + group] = right[strip + group] - weight * row_right
        last = first + STRIP * (LOOK + 1)
        if last < size:
            if strip > 0:
                z_ref[first - STRIP : first, :] = jnp.zeros((STRIP, 2 * size), F32)
            z_ref[first:after, 0:size] = left[strip]
            z_ref[first:after, size : 2 * size] = right[strip]
            update = dot_x3(w_ref[last:size, 0:size], z_ref[...], NN)
            w_ref[last:size, :] = w_ref[last:size, :] - update


def row_of(column):
    return jnp.transpose(jnp.broadcast_to(column, (PANEL, PANEL)))[0:1, :]


def window_kernel(
    noise_ref,
    pivots_ref,
    scale_ref,
    active_ref,
    mine_ref,
    other_ref,
    points_ref,
    prior_ref,
    new_hbm,
    diag_ref,
    g_ref,
    k_ref,
    w_ref,
    z_ref,
    inv_ref,
    x_ref,
    out_sems,
):
    rows = points_ref.shape[0]
    homes = mine_ref.shape[0]
    index = lax.axis_index("rows")
    core = lax.rem(index, 2)
    base = index * rows
    noise = noise_ref[0]
    scale = scale_ref[...]
    for ref, half in ((mine_ref, core), (other_ref, 1 - core)):
        for turn in range(HALF // homes):
            at = pl.ds(pl.multiple_of(half * HALF, HALF) + turn * homes, homes)
            g_ref[at, :] = ref[:, 0, turn * F : (turn + 1) * F]
    order = pivot_order(pivots_ref)
    lane = lax.broadcasted_iota(jnp.int32, (1, PIV), 1)
    half, turn, home = lane // HALF, lane % HALF // homes, lane % homes
    held = (2 * home + half + 2 * homes * turn).astype(F32)
    place = (order == held).astype(BF)
    pp2 = [dot_bf(place, part, NN) for part in split2(g_ref[:, 0:D] * scale)]
    pp = pp2[0] + pp2[1]
    pp2 = [part.astype(BF) for part in pp2]
    pf2 = [dot_bf(place, part, NN).astype(BF) for part in split2(g_ref[:, D:F])]
    square_col = jnp.sum(pp * pp, axis=1, keepdims=True)
    square_row = jnp.concatenate(
        [row_of(square_col[i * PANEL : (i + 1) * PANEL]) for i in range(PANELS)], axis=1
    )
    eye = (
        lax.broadcasted_iota(jnp.int32, (PIV, PIV), 0)
        == lax.broadcasted_iota(jnp.int32, (PIV, PIV), 1)
    ).astype(F32)
    for low, high in ((0, 2 * PANEL), (2 * PANEL, PIV)):
        down = [slice(low, PIV), slice(low, high)]
        inner = three([part[down[0]] for part in pp2], [part[down[1]] for part in pp2])
        gram = jnp.exp(-0.5 * (square_col[down[0]] + square_row[:, down[1]] - 2.0 * inner))
        gram = gram + noise * eye[down[0], down[1]]
        k_ref[down[0], down[1]] = gram - three(
            [part[down[0]] for part in pf2], [part[down[1]] for part in pf2]
        )
    mine = points_ref[...] * scale
    prior = prior_ref[...]
    mine_col = jnp.sum(mine * mine, axis=1, keepdims=True)
    residual = jnp.exp(-0.5 * (mine_col + square_row - 2.0 * three(split2(mine), pp2)))
    residual = residual - three(split2(prior), pf2)
    ids = base + lax.broadcasted_iota(jnp.int32, (rows, PANEL), 0)
    for panel in range(PANELS):
        span = slice(panel * PANEL, (panel + 1) * PANEL)
        same = (ids == pivots_ref[panel : panel + 1, :]).astype(F32)
        x_ref[:, span] = residual[:, span] + noise * same
    small_eye = eye[0:PANEL, 0:PANEL]
    total = jnp.sum(prior * prior, axis=1, keepdims=True)
    stores = []
    for panel in range(PANELS):
        span = slice(panel * PANEL, (panel + 1) * PANEL)
        w_ref[:, 0:PANEL] = k_ref[span, span]
        w_ref[:, PANEL:] = small_eye
        factor(w_ref, z_ref, inv_ref)
        inverse = split2(inv_ref[...])
        if panel + 1 < PANELS:
            rest = slice((panel + 1) * PANEL, PIV)
            below = split2(three(split2(k_ref[rest, span]), inverse))
            k_ref[rest, rest] = k_ref[rest, rest] - three(below, below)
        fresh = three(split2(x_ref[:, span]), inverse)
        mask = jnp.concatenate(
            [
                column_of(active_ref[panel : panel + 1, i * 128 : (i + 1) * 128].astype(F32))
                for i in range(rows // 128)
            ],
            axis=0,
        )
        fresh = fresh * mask
        x_ref[:, span] = fresh
        store = pltpu.make_async_copy(x_ref.at[:, span], new_hbm.at[:, span], out_sems.at[panel])
        store.start()
        stores.append(store)
        total = total + jnp.sum(fresh * fresh, axis=1, keepdims=True)
        if panel + 1 < PANELS:
            x_ref[:, rest] = x_ref[:, rest] - three(split2(fresh), below)
    diag = (1.0 + noise) - total
    for i in range(rows // 128):
        diag_ref[i * 128 : (i + 1) * 128] = row_of(diag[i * 128 : (i + 1) * 128])[0]
    for store in stores:
        store.wait()


SMEM = pl.BlockSpec(memory_space=pltpu.SMEM)
VMEM = pl.BlockSpec(memory_space=pltpu.VMEM)
SMALL = pltpu.CompilerParams(vmem_limit_bytes=16 * 1024 * 1024)
ANY = pl.BlockSpec(memory_space=pl.ANY)
HBM = pl.BlockSpec(memory_space=pltpu.HBM)


def local(points, inv_scale, noise, prior, active, pivots):
    rows = points.shape[0]
    devices = lax.axis_size("rows")
    homes = devices // 2
    partner = [(i, i ^ 1) for i in range(devices)]
    groups = [[2 * chip + core for chip in range(homes)] for core in range(2)]
    exchange = functools.partial(
        lax.all_to_all, axis_name="rows", split_axis=0, concat_axis=0, tiled=True
    )
    def routed(turn, pivots):
        send, pick, turns, kept = pl.pallas_call(
            pack_kernel,
            out_shape=(
                jax.ShapeDtypeStruct((devices, 1, F), F32),
                jax.ShapeDtypeStruct((8, devices), F32),
                jax.ShapeDtypeStruct((1,), jnp.int32),
                jax.ShapeDtypeStruct((PANELS, PANEL), jnp.int32),
            ),
            in_specs=[SMEM, VMEM, HBM, HBM],
            out_specs=(VMEM, VMEM, SMEM, VMEM),
            scratch_shapes=[
                pltpu.VMEM((rows, D), F32),
                pltpu.VMEM((rows, R0), F32),
                pltpu.SemaphoreType.DMA((2,)),
            ],
            name="pack",
            compiler_params=SMALL,
        )(turn, pivots, points, prior)
        owned = pl.pallas_call(
            pick_kernel,
            out_shape=jax.ShapeDtypeStruct((1, 1, PIV // devices * F), F32),
            in_specs=[VMEM, VMEM],
            out_specs=VMEM,
            scratch_shapes=[pltpu.VMEM((devices, F), F32)],
            name="pick",
            compiler_params=SMALL,
        )(pick, exchange(send))
        return owned, turns[0], kept

    owned, turns, pivots = routed(jnp.zeros((1,), jnp.int32), pivots)

    def more(state):
        return state[0] < turns

    def again(state):
        turn, owned = state
        return turn + 1, owned + routed(turn[None], pivots)[0]

    owned = lax.while_loop(more, again, (jnp.int32(1), owned))[1]
    mine = exchange(jnp.broadcast_to(owned, (homes, *owned.shape[1:])), axis_index_groups=groups)
    other = lax.ppermute(mine, "rows", partner)
    return pl.pallas_call(
        window_kernel,
        out_shape=(
            jax.ShapeDtypeStruct((rows, PIV), F32),
            jax.ShapeDtypeStruct((rows,), F32),
        ),
        in_specs=[SMEM] + [VMEM] * 7,
        out_specs=(ANY, VMEM),
        scratch_shapes=[
            pltpu.VMEM((PIV, F), F32),
            pltpu.VMEM((PIV, PIV), F32),
            pltpu.VMEM((PANEL, 2 * PANEL), F32),
            pltpu.VMEM((PANEL, 2 * PANEL), F32),
            pltpu.VMEM((PANEL, PANEL), F32),
            pltpu.VMEM((rows, PIV), F32),
            pltpu.SemaphoreType.DMA((PANELS,)),
        ],
        name="window",
        compiler_params=SMALL,
    )(noise, pivots, inv_scale.reshape(1, D), active, mine, other, points, prior)


def solution(mesh):
    return jax.shard_map(
        local,
        mesh=mesh,
        in_specs=(P("rows", None), P(), P(), P("rows", None), P(None, "rows"), P()),
        out_specs=(P("rows", None), P("rows")),
        check_vma=False,
    )
```

```python
import functools

import jax
import jax.numpy as jnp
from jax import lax
from jax.experimental import pallas as pl
from jax.experimental.pallas import tpu as pltpu
from jax.sharding import PartitionSpec as P

D = 256
R0 = 512
F = D + R0
PANEL = 128
PANELS = 3
PIV = PANEL * PANELS
FAR = 1e9
HALF = PIV // 2
STRIP = 8
LOOK = 2
BF = jnp.bfloat16
F32 = jnp.float32
NT = (((1,), (1,)), ((), ()))
NN = (((1,), (0,)), ((), ()))


def split2(a):
    high = a.astype(BF)
    return high, (a - high.astype(F32)).astype(BF)


def split3(a):
    high = a.astype(BF)
    rest = a - high.astype(F32)
    mid = rest.astype(BF)
    return high, mid, (rest - mid.astype(F32)).astype(BF)


def dot_bf(a, b, dims=NT):
    return lax.dot_general(a, b, dims, preferred_element_type=F32)


def dot_x3(a, b, dims=NT):
    return three(split2(a), split2(b), dims)


def three(a, b, dims=NT):
    return dot_bf(a[0], b[0], dims) + (dot_bf(a[0], b[1], dims) + dot_bf(a[1], b[0], dims))


def column_of(row):
    return jnp.transpose(jnp.broadcast_to(row, (8, 128)))[:, 0:1]


def pivot_columns(pivots_ref):
    return [column_of(pivots_ref[p : p + 1, :].astype(F32)) for p in range(PANELS)]


def halves(parts):
    cut = PANEL // 2
    return (
        [parts[0], parts[1][0:cut]],
        [parts[1][cut:PANEL], parts[2]],
    )


def place_in_half(pivots_ref, half):
    lane = lax.broadcasted_iota(jnp.int32, (1, PANEL), 1)
    rows = [pivots_ref[p : p + 1, :].astype(F32) for p in range(PANELS)]
    mixed = jnp.where((lane < PANEL // 2) == (half == 0), rows[1], FAR)
    order = []
    for column in halves(pivot_columns(pivots_ref))[half]:
        ahead = (rows[2 * half] < column).astype(F32) + (mixed < column).astype(F32)
        order.append(jnp.sum(ahead, axis=1, keepdims=True))
    order = jnp.concatenate(order, axis=0)
    held = lax.broadcasted_iota(jnp.int32, (HALF, HALF), 1).astype(F32)
    return (order == held).astype(BF)


def count_halves(tests):
    return sum(jnp.sum(test.astype(F32), axis=0, keepdims=True) for test in tests)


def pack_kernel(
    turn_ref,
    pivots_ref,
    points_hbm,
    prior_hbm,
    send_ref,
    pick_ref,
    turns_ref,
    kept_ref,
    points_ref,
    prior_ref,
    sems,
):
    loads = [
        pltpu.make_async_copy(source, target, sems.at[i])
        for i, (source, target) in enumerate(
            ((points_hbm, points_ref), (prior_hbm, prior_ref))
        )
    ]
    for load in loads:
        load.start()
    rows = points_ref.shape[0]
    devices = send_ref.shape[0]
    index = lax.axis_index("rows")
    turn = turn_ref[0].astype(F32)
    base = (index * rows).astype(F32)
    kept_ref[...] = pivots_ref[...]
    ids = base + lax.broadcasted_iota(jnp.int32, (1, rows), 1).astype(F32)
    homes = devices // 2
    target = lax.broadcasted_iota(jnp.int32, (devices, rows), 0).astype(F32)
    edges = rows * lax.broadcasted_iota(jnp.int32, (1, devices), 1).astype(F32)
    slot = lax.broadcasted_iota(jnp.int32, (8, devices), 0)
    core = lax.rem(index, 2)
    wanted = (index // 2).astype(F32) + homes * slot.astype(F32)
    select, pick, longest = None, None, None
    for half, columns in enumerate(halves(pivot_columns(pivots_ref))):
        place = count_halves([column < ids for column in columns])
        found = count_halves([column == ids for column in columns])
        step = place - place[:, 0:1] - homes * turn
        home = 2.0 * (place - homes * jnp.floor(place * (1.0 / homes))) + half
        home = jnp.where((found > 0.5) & (step >= 0.0) & (step < homes), home, -1.0)
        start = count_halves([column < edges for column in columns])
        stop = count_halves([column < edges + rows for column in columns])
        step = wanted - start - homes * turn
        mine = (wanted >= start) & (wanted < stop) & (step >= 0.0) & (step < homes)
        mine = mine & (slot < HALF // homes) & (core == half)
        hit = target == home
        run = jnp.max(stop - start)
        select = hit if half == 0 else select | hit
        pick = mine if half == 0 else pick | mine
        longest = run if half == 0 else jnp.maximum(longest, run)
    select = select.astype(BF)
    pick_ref[...] = pick.astype(F32)
    turns_ref[0] = jnp.where(longest > 2 * homes, 3, jnp.where(longest > homes, 2, 1))
    at = 0
    for load, ref in ((loads[0], points_ref), (loads[1], prior_ref)):
        load.wait()
        high, mid, low = split3(ref[...])
        got = dot_bf(select, high, NN) + dot_bf(select, mid, NN) + dot_bf(select, low, NN)
        send_ref[:, 0, at : at + got.shape[1]] = got
        at += got.shape[1]


def pick_kernel(pick_ref, came_ref, out_ref, rows_ref):
    rows_ref[...] = came_ref[:, 0, :]
    select = pick_ref[...].astype(BF)
    high, mid, low = split3(rows_ref[...])
    got = dot_bf(select, high, NN) + dot_bf(select, mid, NN) + dot_bf(select, low, NN)
    for row in range(out_ref.shape[2] // F):
        out_ref[0, :, row * F : (row + 1) * F] = got[row : row + 1, :]


def spread_lane(block, lane):
    return jnp.broadcast_to(block[:, lane : lane + 1], (STRIP, PANEL))


def spread_row(block, row):
    return jnp.broadcast_to(block[row : row + 1, :], (STRIP, PANEL))


def factor(w_ref, z_ref, inv_ref):
    size = PANEL
    strips = size // STRIP
    iota = lax.broadcasted_iota(jnp.int32, (STRIP, size), 0)
    z_ref[...] = jnp.zeros_like(z_ref)
    left, right, ready = {}, {}, {}
    for strip in range(strips):
        first = STRIP * strip
        after = first + STRIP
        groups = range(min(LOOK + 1, strips - strip))
        for group in groups:
            if strip + group not in left:
                rows = slice(first + STRIP * group, after + STRIP * group)
                left[strip + group] = w_ref[rows, 0:size]
                right[strip + group] = w_ref[rows, size : 2 * size]
        column = {}
        for group in groups:
            for j in range(STRIP):
                if group == 0 and strip > 0:
                    column[group, j] = ready[j]
                else:
                    column[group, j] = spread_lane(left[strip + group], first + j)
        ready = {}
        if strip + 1 < strips:
            ready = {m: spread_lane(left[strip + 1], after + m) for m in range(STRIP)}
        for j in range(STRIP):
            root = lax.rsqrt(spread_row(column[0, j], j))
            inverse = root * root
            row_left = spread_row(left[strip], j)
            row_right = spread_row(right[strip], j)
            inv_ref[first + j : first + j + 1, :] = row_right[0:1] * root[0:1]
            own = {m: spread_row(column[0, m], j) for m in range(j + 1, STRIP)}
            ahead = {m: spread_row(column[1, j], m) for m in ready}
            for group in groups:
                weight = column[group, j] * inverse
                if group == 0:
                    weight = jnp.where(iota == j, 1.0 - inverse, weight)
                for m in own:
                    column[group, m] = column[group, m] - weight * own[m]
                if group == 1:
                    for m in ready:
                        ready[m] = ready[m] - weight * ahead[m]
                left[strip + group] = left[strip + group] - weight * row_left
                right[strip + group] = right[strip + group] - weight * row_right
        last = first + STRIP * (LOOK + 1)
        if last < size:
            if strip > 0:
                z_ref[first - STRIP : first, :] = jnp.zeros((STRIP, 2 * size), F32)
            z_ref[first:after, 0:size] = left[strip]
            z_ref[first:after, size : 2 * size] = right[strip]
            update = dot_x3(w_ref[last:size, 0:size], z_ref[...], NN)
            w_ref[last:size, :] = w_ref[last:size, :] - update


def row_of(column):
    return jnp.transpose(jnp.broadcast_to(column, (PANEL, PANEL)))[0:1, :]


def prepare_kernel(
    pivots_ref, scale_ref, points_ref, prior_ref, mine_ref, prior2_ref, sums_ref, place_ref
):
    mine = points_ref[...] * scale_ref[...]
    prior = prior_ref[...]
    for ref, value in ((mine_ref, mine), (prior2_ref, prior)):
        ref[0], ref[1] = split2(value)
    for row, value in enumerate((mine, prior)):
        total = jnp.sum(value * value, axis=1, keepdims=True)
        for i in range(value.shape[0] // 128):
            here = slice(i * 128, (i + 1) * 128)
            sums_ref[row : row + 1, here] = row_of(total[here])
    for half in range(2):
        place_ref[half] = place_in_half(pivots_ref, half)


def half_of(half, noise, pivots_ref, scale_ref, place_ref, sums_ref, mine_ref, prior_ref, buf_ref, g_ref):
    homes = buf_ref.shape[0]
    rows = mine_ref.shape[1]
    for turn in range(HALF // homes):
        g_ref[turn * homes : (turn + 1) * homes, :] = buf_ref[:, 0, turn * F : (turn + 1) * F]
    place = place_ref[half]
    near = [dot_bf(place, part, NN) for part in split2(g_ref[:, 0:D] * scale_ref[...])]
    both = near[0] + near[1]
    near = [part.astype(BF) for part in near]
    factor_rows = [dot_bf(place, part, NN).astype(BF) for part in split2(g_ref[:, D:F])]
    square = jnp.sum(both * both, axis=1, keepdims=True)
    inner = three(near, (mine_ref[0], mine_ref[1]))
    residual = jnp.exp(-0.5 * (square + sums_ref[0:1, :] - 2.0 * inner))
    residual = residual - three(factor_rows, (prior_ref[0], prior_ref[1]))
    first, second = halves(pivot_columns(pivots_ref))
    wanted = jnp.where(half == 0, jnp.concatenate(first, 0), jnp.concatenate(second, 0))
    ids = lax.axis_index("rows") * rows + lax.broadcasted_iota(jnp.int32, (1, rows), 1)
    residual = residual + noise * (wanted == ids.astype(F32)).astype(F32)
    return near, factor_rows, square, residual


def half_kernel(
    noise_ref,
    pivots_ref,
    scale_ref,
    place_ref,
    sums_ref,
    mine_ref,
    prior_ref,
    buf_ref,
    near_ref,
    rows_ref,
    square_ref,
    residual_ref,
    g_ref,
):
    half = lax.rem(lax.axis_index("rows"), 2)
    near, factor_rows, square, residual = half_of(
        half,
        noise_ref[0],
        pivots_ref,
        scale_ref,
        place_ref,
        sums_ref,
        mine_ref,
        prior_ref,
        buf_ref,
        g_ref,
    )
    for part in range(2):
        near_ref[part] = near[part]
        rows_ref[part] = factor_rows[part]
    square_ref[...] = square
    residual_ref[...] = residual


def window_kernel(
    noise_ref,
    pivots_ref,
    scale_ref,
    place_ref,
    sums_ref,
    mine_ref,
    prior_ref,
    buf_ref,
    own_near_ref,
    own_rows_ref,
    own_square_ref,
    own_residual_ref,
    active_ref,
    new_hbm,
    diag_ref,
    near_ref,
    rows_ref,
    square_ref,
    r_ref,
    g_ref,
    k_ref,
    w_ref,
    z_ref,
    inv_ref,
    x_ref,
    out_sems,
):
    rows = mine_ref.shape[1]
    noise = noise_ref[0]
    core = lax.rem(lax.axis_index("rows"), 2)
    here = pl.ds(pl.multiple_of(core * HALF, HALF), HALF)
    there = pl.ds(pl.multiple_of((1 - core) * HALF, HALF), HALF)
    near, factor_rows, square, residual = half_of(
        1 - core,
        noise,
        pivots_ref,
        scale_ref,
        place_ref,
        sums_ref,
        mine_ref,
        prior_ref,
        buf_ref,
        g_ref,
    )
    for part in range(2):
        near_ref[part, here, :] = own_near_ref[part]
        near_ref[part, there, :] = near[part]
        rows_ref[part, here, :] = own_rows_ref[part]
        rows_ref[part, there, :] = factor_rows[part]
    square_ref[here, :] = own_square_ref[...]
    square_ref[there, :] = square
    r_ref[here, :] = own_residual_ref[...]
    r_ref[there, :] = residual
    square_col = square_ref[...]
    square_row = jnp.concatenate(
        [row_of(square_col[i * PANEL : (i + 1) * PANEL]) for i in range(PANELS)], axis=1
    )
    eye = (
        lax.broadcasted_iota(jnp.int32, (PIV, PIV), 0)
        == lax.broadcasted_iota(jnp.int32, (PIV, PIV), 1)
    ).astype(F32)
    for low, high in ((0, 2 * PANEL), (2 * PANEL, PIV)):
        down, over = slice(low, PIV), slice(low, high)
        inner = three(
            (near_ref[0, down, :], near_ref[1, down, :]),
            (near_ref[0, over, :], near_ref[1, over, :]),
        )
        gram = jnp.exp(-0.5 * (square_col[down] + square_row[:, over] - 2.0 * inner))
        k_ref[down, over] = (gram + noise * eye[down, over]) - three(
            (rows_ref[0, down, :], rows_ref[1, down, :]),
            (rows_ref[0, over, :], rows_ref[1, over, :]),
        )
    small_eye = eye[0:PANEL, 0:PANEL]
    total = sums_ref[1:2, :]
    stores = []
    for panel in range(PANELS):
        span = slice(panel * PANEL, (panel + 1) * PANEL)
        w_ref[:, 0:PANEL] = k_ref[span, span]
        w_ref[:, PANEL:] = small_eye
        factor(w_ref, z_ref, inv_ref)
        inverse = split2(inv_ref[...])
        if panel + 1 < PANELS:
            rest = slice((panel + 1) * PANEL, PIV)
            below = split2(three(split2(k_ref[rest, span]), inverse))
            k_ref[rest, rest] = k_ref[rest, rest] - three(below, below)
        fresh = three(inverse, split2(r_ref[span, :]), NN)
        fresh = fresh * active_ref[panel : panel + 1, :].astype(F32)
        total = total + jnp.sum(fresh * fresh, axis=0, keepdims=True)
        x_ref[:, span] = jnp.transpose(fresh)
        store = pltpu.make_async_copy(x_ref.at[:, span], new_hbm.at[:, span], out_sems.at[panel])
        store.start()
        stores.append(store)
        if panel + 1 < PANELS:
            r_ref[rest, :] = r_ref[rest, :] - three(below, split2(fresh), NN)
    diag = (1.0 + noise) - total
    for i in range(rows // 128):
        span = slice(i * 128, (i + 1) * 128)
        diag_ref[span] = diag[0, span]
    for store in stores:
        store.wait()


SMEM = pl.BlockSpec(memory_space=pltpu.SMEM)
VMEM = pl.BlockSpec(memory_space=pltpu.VMEM)
SMALL = pltpu.CompilerParams(vmem_limit_bytes=16 * 1024 * 1024)
ANY = pl.BlockSpec(memory_space=pl.ANY)
HBM = pl.BlockSpec(memory_space=pltpu.HBM)


def local(points, inv_scale, noise, prior, active, pivots):
    rows = points.shape[0]
    devices = lax.axis_size("rows")
    homes = devices // 2
    partner = [(i, i ^ 1) for i in range(devices)]
    groups = [[2 * chip + core for chip in range(homes)] for core in range(2)]
    exchange = functools.partial(
        lax.all_to_all, axis_name="rows", split_axis=0, concat_axis=0, tiled=True
    )
    def routed(turn, pivots):
        send, pick, turns, kept = pl.pallas_call(
            pack_kernel,
            out_shape=(
                jax.ShapeDtypeStruct((devices, 1, F), F32),
                jax.ShapeDtypeStruct((8, devices), F32),
                jax.ShapeDtypeStruct((1,), jnp.int32),
                jax.ShapeDtypeStruct((PANELS, PANEL), jnp.int32),
            ),
            in_specs=[SMEM, VMEM, HBM, HBM],
            out_specs=(VMEM, VMEM, SMEM, VMEM),
            scratch_shapes=[
                pltpu.VMEM((rows, D), F32),
                pltpu.VMEM((rows, R0), F32),
                pltpu.SemaphoreType.DMA((2,)),
            ],
            name="pack",
            compiler_params=SMALL,
        )(turn, pivots, points, prior)
        owned = pl.pallas_call(
            pick_kernel,
            out_shape=jax.ShapeDtypeStruct((1, 1, PIV // devices * F), F32),
            in_specs=[VMEM, VMEM],
            out_specs=VMEM,
            scratch_shapes=[pltpu.VMEM((devices, F), F32)],
            name="pick",
            compiler_params=SMALL,
        )(pick, exchange(send))
        return owned, turns[0], kept

    owned, turns, pivots = routed(jnp.zeros((1,), jnp.int32), pivots)

    scale = inv_scale.reshape(1, D)
    mine2, prior2, sums, place = pl.pallas_call(
        prepare_kernel,
        out_shape=(
            jax.ShapeDtypeStruct((2, rows, D), BF),
            jax.ShapeDtypeStruct((2, rows, R0), BF),
            jax.ShapeDtypeStruct((2, rows), F32),
            jax.ShapeDtypeStruct((2, HALF, HALF), BF),
        ),
        in_specs=[VMEM] * 4,
        out_specs=(VMEM,) * 4,
        name="prepare",
        compiler_params=SMALL,
    )(pivots, scale, points, prior)
    owned, mine2, prior2, sums, place = lax.optimization_barrier(
        (owned, mine2, prior2, sums, place)
    )

    def more(state):
        return state[0] < turns

    def again(state):
        turn, owned = state
        return turn + 1, owned + routed(turn[None], pivots)[0]

    owned = lax.while_loop(more, again, (jnp.int32(1), owned))[1]
    mine = exchange(jnp.broadcast_to(owned, (homes, *owned.shape[1:])), axis_index_groups=groups)
    other = lax.ppermute(mine, "rows", partner)
    common = (noise, pivots, scale, place, sums, mine2, prior2)
    own = pl.pallas_call(
        half_kernel,
        out_shape=(
            jax.ShapeDtypeStruct((2, HALF, D), BF),
            jax.ShapeDtypeStruct((2, HALF, R0), BF),
            jax.ShapeDtypeStruct((HALF, 1), F32),
            jax.ShapeDtypeStruct((HALF, rows), F32),
        ),
        in_specs=[SMEM] + [VMEM] * 7,
        out_specs=(VMEM,) * 4,
        scratch_shapes=[pltpu.VMEM((HALF, F), F32)],
        name="half",
        compiler_params=SMALL,
    )(*common, mine)
    return pl.pallas_call(
        window_kernel,
        out_shape=(
            jax.ShapeDtypeStruct((rows, PIV), F32),
            jax.ShapeDtypeStruct((rows,), F32),
        ),
        in_specs=[SMEM] + [VMEM] * 12,
        out_specs=(ANY, VMEM),
        scratch_shapes=[
            pltpu.VMEM((2, PIV, D), BF),
            pltpu.VMEM((2, PIV, R0), BF),
            pltpu.VMEM((PIV, 1), F32),
            pltpu.VMEM((PIV, rows), F32),
            pltpu.VMEM((HALF, F), F32),
            pltpu.VMEM((PIV, PIV), F32),
            pltpu.VMEM((PANEL, 2 * PANEL), F32),
            pltpu.VMEM((PANEL, 2 * PANEL), F32),
            pltpu.VMEM((PANEL, PANEL), F32),
            pltpu.VMEM((rows, PIV), F32),
            pltpu.SemaphoreType.DMA((PANELS,)),
        ],
        name="window",
        compiler_params=SMALL,
    )(*common, other, *own, active)


def solution(mesh):
    return jax.shard_map(
        local,
        mesh=mesh,
        in_specs=(P("rows", None), P(), P(), P("rows", None), P(None, "rows"), P()),
        out_specs=(P("rows", None), P("rows")),
        check_vma=False,
    )
```

```python
import functools

import jax
import jax.numpy as jnp
from jax import lax
from jax.experimental import pallas as pl
from jax.experimental.pallas import tpu as pltpu
from jax.sharding import PartitionSpec as P

D = 256
R0 = 512
F = D + R0
PANEL = 128
PANELS = 3
PIV = PANEL * PANELS
FAR = 1e9
HALF = PIV // 2
STRIP = 8
LOOK = 2
BF = jnp.bfloat16
F32 = jnp.float32
NT = (((1,), (1,)), ((), ()))
NN = (((1,), (0,)), ((), ()))


def split2(a):
    high = a.astype(BF)
    return high, (a - high.astype(F32)).astype(BF)


def split3(a):
    high = a.astype(BF)
    rest = a - high.astype(F32)
    mid = rest.astype(BF)
    return high, mid, (rest - mid.astype(F32)).astype(BF)


def dot_bf(a, b, dims=NT):
    return lax.dot_general(a, b, dims, preferred_element_type=F32)


def dot_x3(a, b, dims=NT):
    return three(split2(a), split2(b), dims)


def three(a, b, dims=NT):
    return dot_bf(a[0], b[0], dims) + (dot_bf(a[0], b[1], dims) + dot_bf(a[1], b[0], dims))


def column_of(row):
    return jnp.transpose(jnp.broadcast_to(row, (8, 128)))[:, 0:1]


def pivot_columns(pivots_ref):
    return [column_of(pivots_ref[p : p + 1, :].astype(F32)) for p in range(PANELS)]


def halves(parts):
    cut = PANEL // 2
    return (
        [parts[0], parts[1][0:cut]],
        [parts[1][cut:PANEL], parts[2]],
    )


def place_in_half(pivots_ref, half):
    lane = lax.broadcasted_iota(jnp.int32, (1, PANEL), 1)
    rows = [pivots_ref[p : p + 1, :].astype(F32) for p in range(PANELS)]
    mixed = jnp.where((lane < PANEL // 2) == (half == 0), rows[1], FAR)
    order = []
    for column in halves(pivot_columns(pivots_ref))[half]:
        ahead = (rows[2 * half] < column).astype(F32) + (mixed < column).astype(F32)
        order.append(jnp.sum(ahead, axis=1, keepdims=True))
    order = jnp.concatenate(order, axis=0)
    held = lax.broadcasted_iota(jnp.int32, (HALF, HALF), 1).astype(F32)
    return (order == held).astype(BF)


def count_halves(tests):
    return sum(jnp.sum(test.astype(F32), axis=0, keepdims=True) for test in tests)


def pack_kernel(
    turn_ref,
    pivots_hbm,
    points_hbm,
    prior_hbm,
    send_hbm,
    pick_ref,
    turns_ref,
    pivots_ref,
    points_ref,
    prior_ref,
    send_ref,
    sems,
    out_sems,
):
    loads = [
        pltpu.make_async_copy(source, target, sems.at[i])
        for i, (source, target) in enumerate(
            ((pivots_hbm, pivots_ref), (points_hbm, points_ref), (prior_hbm, prior_ref))
        )
    ]
    for load in loads:
        load.start()
    rows = points_ref.shape[0]
    devices = send_ref.shape[0]
    index = lax.axis_index("rows")
    turn = turn_ref[0].astype(F32)
    base = (index * rows).astype(F32)
    loads[0].wait()
    ids = base + lax.broadcasted_iota(jnp.int32, (1, rows), 1).astype(F32)
    homes = devices // 2
    target = lax.broadcasted_iota(jnp.int32, (devices, rows), 0).astype(F32)
    edges = rows * lax.broadcasted_iota(jnp.int32, (1, devices), 1).astype(F32)
    slot = lax.broadcasted_iota(jnp.int32, (8, devices), 0)
    core = lax.rem(index, 2)
    wanted = (index // 2).astype(F32) + homes * slot.astype(F32)
    select, pick, longest = None, None, None
    for half, columns in enumerate(halves(pivot_columns(pivots_ref))):
        place = count_halves([column < ids for column in columns])
        found = count_halves([column == ids for column in columns])
        step = place - place[:, 0:1] - homes * turn
        home = 2.0 * (place - homes * jnp.floor(place * (1.0 / homes))) + half
        home = jnp.where((found > 0.5) & (step >= 0.0) & (step < homes), home, -1.0)
        start = count_halves([column < edges for column in columns])
        stop = count_halves([column < edges + rows for column in columns])
        step = wanted - start - homes * turn
        mine = (wanted >= start) & (wanted < stop) & (step >= 0.0) & (step < homes)
        mine = mine & (slot < HALF // homes) & (core == half)
        hit = target == home
        run = jnp.max(stop - start)
        select = hit if half == 0 else select | hit
        pick = mine if half == 0 else pick | mine
        longest = run if half == 0 else jnp.maximum(longest, run)
    select = select.astype(BF)
    pick_ref[...] = pick.astype(F32)
    turns_ref[0] = jnp.where(longest > 2 * homes, 3, jnp.where(longest > homes, 2, 1))
    at = 0
    stores = []
    for load, ref in ((loads[1], points_ref), (loads[2], prior_ref)):
        load.wait()
        high, mid, low = split3(ref[...])
        got = dot_bf(select, high, NN) + dot_bf(select, mid, NN) + dot_bf(select, low, NN)
        span = slice(at, at + got.shape[1])
        send_ref[:, 0, span] = got
        at += got.shape[1]
        stores.append(
            pltpu.make_async_copy(
                send_ref.at[:, :, span], send_hbm.at[:, :, span], out_sems.at[len(stores)]
            )
        )
        stores[-1].start()
    for store in stores:
        store.wait()


def pick_kernel(pick_ref, came_ref, out_ref, rows_ref):
    rows_ref[...] = came_ref[:, 0, :]
    select = pick_ref[...].astype(BF)
    high, mid, low = split3(rows_ref[...])
    got = dot_bf(select, high, NN) + dot_bf(select, mid, NN) + dot_bf(select, low, NN)
    for row in range(out_ref.shape[2] // F):
        out_ref[0, :, row * F : (row + 1) * F] = got[row : row + 1, :]


def spread_lane(block, lane):
    return jnp.broadcast_to(block[:, lane : lane + 1], (STRIP, PANEL))


def spread_row(block, row):
    return jnp.broadcast_to(block[row : row + 1, :], (STRIP, PANEL))


def factor(w_ref, z_ref, inv_ref):
    size = PANEL
    strips = size // STRIP
    iota = lax.broadcasted_iota(jnp.int32, (STRIP, size), 0)
    z_ref[...] = jnp.zeros_like(z_ref)
    left, right, ready = {}, {}, {}
    for strip in range(strips):
        first = STRIP * strip
        after = first + STRIP
        groups = range(min(LOOK + 1, strips - strip))
        for group in groups:
            if strip + group not in left:
                rows = slice(first + STRIP * group, after + STRIP * group)
                left[strip + group] = w_ref[rows, 0:size]
                right[strip + group] = w_ref[rows, size : 2 * size]
        column = {}
        for group in groups:
            for j in range(STRIP):
                if group == 0 and strip > 0:
                    column[group, j] = ready[j]
                else:
                    column[group, j] = spread_lane(left[strip + group], first + j)
        ready = {}
        if strip + 1 < strips:
            ready = {m: spread_lane(left[strip + 1], after + m) for m in range(STRIP)}
        for j in range(STRIP):
            root = lax.rsqrt(spread_row(column[0, j], j))
            inverse = root * root
            row_left = spread_row(left[strip], j)
            row_right = spread_row(right[strip], j)
            inv_ref[first + j : first + j + 1, :] = row_right[0:1] * root[0:1]
            own = {m: spread_row(column[0, m], j) for m in range(j + 1, STRIP)}
            ahead = {m: spread_row(column[1, j], m) for m in ready}
            for group in groups:
                weight = column[group, j] * inverse
                if group == 0:
                    weight = jnp.where(iota == j, 1.0 - inverse, weight)
                for m in own:
                    column[group, m] = column[group, m] - weight * own[m]
                if group == 1:
                    for m in ready:
                        ready[m] = ready[m] - weight * ahead[m]
                left[strip + group] = left[strip + group] - weight * row_left
                right[strip + group] = right[strip + group] - weight * row_right
        last = first + STRIP * (LOOK + 1)
        if last < size:
            if strip > 0:
                z_ref[first - STRIP : first, :] = jnp.zeros((STRIP, 2 * size), F32)
            z_ref[first:after, 0:size] = left[strip]
            z_ref[first:after, size : 2 * size] = right[strip]
            update = dot_x3(w_ref[last:size, 0:size], z_ref[...], NN)
            w_ref[last:size, :] = w_ref[last:size, :] - update


def row_of(column):
    return jnp.transpose(jnp.broadcast_to(column, (PANEL, PANEL)))[0:1, :]


def prepare_kernel(
    pivots_ref,
    scale_ref,
    points_ref,
    prior_ref,
    active_ref,
    mine_ref,
    prior2_ref,
    sums_ref,
    place_ref,
    mask_ref,
):
    mask_ref[...] = active_ref[...].astype(F32)
    mine = points_ref[...] * scale_ref[...]
    prior = prior_ref[...]
    for ref, value in ((mine_ref, mine), (prior2_ref, prior)):
        ref[0], ref[1] = split2(value)
    for row, value in enumerate((mine, prior)):
        total = jnp.sum(value * value, axis=1, keepdims=True)
        for i in range(value.shape[0] // 128):
            here = slice(i * 128, (i + 1) * 128)
            sums_ref[row : row + 1, here] = row_of(total[here])
    for half in range(2):
        place_ref[half] = place_in_half(pivots_ref, half)


def half_of(half, noise, pivots_ref, scale_ref, place_ref, sums_ref, mine_ref, prior_ref, buf_ref, g_ref):
    homes = buf_ref.shape[0]
    rows = mine_ref.shape[1]
    for turn in range(HALF // homes):
        g_ref[turn * homes : (turn + 1) * homes, :] = buf_ref[:, 0, turn * F : (turn + 1) * F]
    place = place_ref[half]
    near = [dot_bf(place, part, NN) for part in split2(g_ref[:, 0:D] * scale_ref[...])]
    both = near[0] + near[1]
    near = [part.astype(BF) for part in near]
    factor_rows = [dot_bf(place, part, NN).astype(BF) for part in split2(g_ref[:, D:F])]
    square = jnp.sum(both * both, axis=1, keepdims=True)
    inner = three(near, (mine_ref[0], mine_ref[1]))
    residual = jnp.exp(-0.5 * (square + sums_ref[0:1, :] - 2.0 * inner))
    residual = residual - three(factor_rows, (prior_ref[0], prior_ref[1]))
    first, second = halves(pivot_columns(pivots_ref))
    wanted = jnp.where(half == 0, jnp.concatenate(first, 0), jnp.concatenate(second, 0))
    ids = lax.axis_index("rows") * rows + lax.broadcasted_iota(jnp.int32, (1, rows), 1)
    residual = residual + noise * (wanted == ids.astype(F32)).astype(F32)
    return near, factor_rows, square, residual


def half_kernel(
    noise_ref,
    pivots_ref,
    scale_ref,
    place_ref,
    sums_ref,
    mine_ref,
    prior_ref,
    buf_ref,
    near_ref,
    rows_ref,
    square_ref,
    residual_ref,
    g_ref,
):
    half = lax.rem(lax.axis_index("rows"), 2)
    near, factor_rows, square, residual = half_of(
        half,
        noise_ref[0],
        pivots_ref,
        scale_ref,
        place_ref,
        sums_ref,
        mine_ref,
        prior_ref,
        buf_ref,
        g_ref,
    )
    for part in range(2):
        near_ref[part] = near[part]
        rows_ref[part] = factor_rows[part]
    square_ref[...] = square
    residual_ref[...] = residual


def window_kernel(
    noise_ref,
    pivots_ref,
    scale_ref,
    place_ref,
    sums_ref,
    mine_ref,
    prior_ref,
    buf_ref,
    own_near_ref,
    own_rows_ref,
    own_square_ref,
    own_residual_ref,
    mask_ref,
    new_hbm,
    diag_ref,
    near_ref,
    rows_ref,
    square_ref,
    r_ref,
    g_ref,
    k_ref,
    w_ref,
    z_ref,
    inv_ref,
    x_ref,
    out_sems,
):
    rows = mine_ref.shape[1]
    noise = noise_ref[0]
    core = lax.rem(lax.axis_index("rows"), 2)
    here = pl.ds(pl.multiple_of(core * HALF, HALF), HALF)
    there = pl.ds(pl.multiple_of((1 - core) * HALF, HALF), HALF)
    near, factor_rows, square, residual = half_of(
        1 - core,
        noise,
        pivots_ref,
        scale_ref,
        place_ref,
        sums_ref,
        mine_ref,
        prior_ref,
        buf_ref,
        g_ref,
    )
    for part in range(2):
        near_ref[part, here, :] = own_near_ref[part]
        near_ref[part, there, :] = near[part]
        rows_ref[part, here, :] = own_rows_ref[part]
        rows_ref[part, there, :] = factor_rows[part]
    square_ref[here, :] = own_square_ref[...]
    square_ref[there, :] = square
    r_ref[here, :] = own_residual_ref[...]
    r_ref[there, :] = residual
    square_col = square_ref[...]
    square_row = jnp.concatenate(
        [row_of(square_col[i * PANEL : (i + 1) * PANEL]) for i in range(PANELS)], axis=1
    )
    eye = (
        lax.broadcasted_iota(jnp.int32, (PIV, PIV), 0)
        == lax.broadcasted_iota(jnp.int32, (PIV, PIV), 1)
    ).astype(F32)
    for low, high in ((0, 2 * PANEL), (2 * PANEL, PIV)):
        down, over = slice(low, PIV), slice(low, high)
        inner = three(
            (near_ref[0, down, :], near_ref[1, down, :]),
            (near_ref[0, over, :], near_ref[1, over, :]),
        )
        gram = jnp.exp(-0.5 * (square_col[down] + square_row[:, over] - 2.0 * inner))
        k_ref[down, over] = (gram + noise * eye[down, over]) - three(
            (rows_ref[0, down, :], rows_ref[1, down, :]),
            (rows_ref[0, over, :], rows_ref[1, over, :]),
        )
    small_eye = eye[0:PANEL, 0:PANEL]
    total = sums_ref[1:2, :]
    stores = []
    for panel in range(PANELS):
        span = slice(panel * PANEL, (panel + 1) * PANEL)
        w_ref[:, 0:PANEL] = k_ref[span, span]
        w_ref[:, PANEL:] = small_eye
        factor(w_ref, z_ref, inv_ref)
        inverse = split2(inv_ref[...])
        if panel + 1 < PANELS:
            rest = slice((panel + 1) * PANEL, PIV)
            below = split2(three(split2(k_ref[rest, span]), inverse))
            k_ref[rest, rest] = k_ref[rest, rest] - three(below, below)
        fresh = three(inverse, split2(r_ref[span, :]), NN)
        fresh = fresh * mask_ref[panel : panel + 1, :]
        total = total + jnp.sum(fresh * fresh, axis=0, keepdims=True)
        x_ref[:, span] = jnp.transpose(fresh)
        store = pltpu.make_async_copy(x_ref.at[:, span], new_hbm.at[:, span], out_sems.at[panel])
        store.start()
        stores.append(store)
        if panel + 1 < PANELS:
            r_ref[rest, :] = r_ref[rest, :] - three(below, split2(fresh), NN)
    diag = (1.0 + noise) - total
    for i in range(rows // 128):
        span = slice(i * 128, (i + 1) * 128)
        diag_ref[span] = diag[0, span]
    for store in stores:
        store.wait()


SMEM = pl.BlockSpec(memory_space=pltpu.SMEM)
VMEM = pl.BlockSpec(memory_space=pltpu.VMEM)
SMALL = pltpu.CompilerParams(vmem_limit_bytes=16 * 1024 * 1024)
ANY = pl.BlockSpec(memory_space=pl.ANY)
HBM = pl.BlockSpec(memory_space=pltpu.HBM)


def local(points, inv_scale, noise, prior, active, pivots):
    rows = points.shape[0]
    devices = lax.axis_size("rows")
    homes = devices // 2
    partner = [(i, i ^ 1) for i in range(devices)]
    groups = [[2 * chip + core for chip in range(homes)] for core in range(2)]
    exchange = functools.partial(
        lax.all_to_all, axis_name="rows", split_axis=0, concat_axis=0, tiled=True
    )
    def routed(turn, pivots):
        send, pick, turns, kept = pl.pallas_call(
            pack_kernel,
            out_shape=(
                jax.ShapeDtypeStruct((devices, 1, F), F32),
                jax.ShapeDtypeStruct((8, devices), F32),
                jax.ShapeDtypeStruct((1,), jnp.int32),
                jax.ShapeDtypeStruct((PANELS, PANEL), jnp.int32),
            ),
            in_specs=[SMEM, HBM, HBM, HBM],
            out_specs=(HBM, VMEM, SMEM, VMEM),
            scratch_shapes=[
                pltpu.VMEM((rows, D), F32),
                pltpu.VMEM((rows, R0), F32),
                pltpu.VMEM((devices, 1, F), F32),
                pltpu.SemaphoreType.DMA((3,)),
                pltpu.SemaphoreType.DMA((2,)),
            ],
            name="pack",
            compiler_params=SMALL,
        )(turn, pivots, points, prior)
        owned = pl.pallas_call(
            pick_kernel,
            out_shape=jax.ShapeDtypeStruct((1, 1, PIV // devices * F), F32),
            in_specs=[VMEM, VMEM],
            out_specs=VMEM,
            scratch_shapes=[pltpu.VMEM((devices, F), F32)],
            name="pick",
            compiler_params=SMALL,
        )(pick, exchange(send))
        return owned, turns[0], kept

    owned, turns, pivots = routed(
        jnp.zeros((1,), jnp.int32), pltpu.with_memory_space_constraint(pivots, pltpu.HBM)
    )

    scale = inv_scale.reshape(1, D)
    mine2, prior2, sums, place, mask = pl.pallas_call(
        prepare_kernel,
        out_shape=(
            jax.ShapeDtypeStruct((2, rows, D), BF),
            jax.ShapeDtypeStruct((2, rows, R0), BF),
            jax.ShapeDtypeStruct((2, rows), F32),
            jax.ShapeDtypeStruct((2, HALF, HALF), BF),
            jax.ShapeDtypeStruct((PANELS, rows), F32),
        ),
        in_specs=[VMEM] * 5,
        out_specs=(VMEM,) * 5,
        name="prepare",
        compiler_params=SMALL,
    )(pivots, scale, points, prior, active)
    owned, mine2, prior2, sums, place, mask = lax.optimization_barrier(
        (owned, mine2, prior2, sums, place, mask)
    )

    def more(state):
        return state[0] < turns

    def again(state):
        turn, owned = state
        return turn + 1, owned + routed(turn[None], pivots)[0]

    owned = lax.while_loop(more, again, (jnp.int32(1), owned))[1]
    mine = exchange(jnp.broadcast_to(owned, (homes, *owned.shape[1:])), axis_index_groups=groups)
    other = lax.ppermute(mine, "rows", partner)
    common = (noise, pivots, scale, place, sums, mine2, prior2)
    own = pl.pallas_call(
        half_kernel,
        out_shape=(
            jax.ShapeDtypeStruct((2, HALF, D), BF),
            jax.ShapeDtypeStruct((2, HALF, R0), BF),
            jax.ShapeDtypeStruct((HALF, 1), F32),
            jax.ShapeDtypeStruct((HALF, rows), F32),
        ),
        in_specs=[SMEM] + [VMEM] * 7,
        out_specs=(VMEM,) * 4,
        scratch_shapes=[pltpu.VMEM((HALF, F), F32)],
        name="half",
        compiler_params=SMALL,
    )(*common, mine)
    return pl.pallas_call(
        window_kernel,
        out_shape=(
            jax.ShapeDtypeStruct((rows, PIV), F32),
            jax.ShapeDtypeStruct((rows,), F32),
        ),
        in_specs=[SMEM] + [VMEM] * 12,
        out_specs=(ANY, VMEM),
        scratch_shapes=[
            pltpu.VMEM((2, PIV, D), BF),
            pltpu.VMEM((2, PIV, R0), BF),
            pltpu.VMEM((PIV, 1), F32),
            pltpu.VMEM((PIV, rows), F32),
            pltpu.VMEM((HALF, F), F32),
            pltpu.VMEM((PIV, PIV), F32),
            pltpu.VMEM((PANEL, 2 * PANEL), F32),
            pltpu.VMEM((PANEL, 2 * PANEL), F32),
            pltpu.VMEM((PANEL, PANEL), F32),
            pltpu.VMEM((rows, PIV), F32),
            pltpu.SemaphoreType.DMA((PANELS,)),
        ],
        name="window",
        compiler_params=SMALL,
    )(*common, other, *own, mask)


def solution(mesh):
    return jax.shard_map(
        local,
        mesh=mesh,
        in_specs=(P("rows", None), P(), P(), P("rows", None), P(None, "rows"), P()),
        out_specs=(P("rows", None), P("rows")),
        check_vma=False,
    )
```

```python
import functools

import jax
import jax.numpy as jnp
from jax import lax
from jax.experimental import pallas as pl
from jax.experimental.pallas import tpu as pltpu
from jax.sharding import PartitionSpec as P

D = 256
R0 = 512
F = D + R0
PANEL = 128
PANELS = 3
PIV = PANEL * PANELS
FAR = 1e9
HALF = PIV // 2
STRIP = 8
LOOK = 2
BF = jnp.bfloat16
F32 = jnp.float32
NT = (((1,), (1,)), ((), ()))
NN = (((1,), (0,)), ((), ()))


def split2(a):
    high = a.astype(BF)
    return high, (a - high.astype(F32)).astype(BF)


def split3(a):
    high = a.astype(BF)
    rest = a - high.astype(F32)
    mid = rest.astype(BF)
    return high, mid, (rest - mid.astype(F32)).astype(BF)


def dot_bf(a, b, dims=NT):
    return lax.dot_general(a, b, dims, preferred_element_type=F32)


def dot_x3(a, b, dims=NT):
    return three(split2(a), split2(b), dims)


def three(a, b, dims=NT):
    return dot_bf(a[0], b[0], dims) + (dot_bf(a[0], b[1], dims) + dot_bf(a[1], b[0], dims))


def column_of(row):
    return jnp.transpose(jnp.broadcast_to(row, (8, 128)))[:, 0:1]


def pivot_columns(pivots_ref):
    return [column_of(pivots_ref[p : p + 1, :].astype(F32)) for p in range(PANELS)]


def halves(parts):
    cut = PANEL // 2
    return (
        [parts[0], parts[1][0:cut]],
        [parts[1][cut:PANEL], parts[2]],
    )


def place_in_half(pivots_ref, half):
    lane = lax.broadcasted_iota(jnp.int32, (1, PANEL), 1)
    rows = [pivots_ref[p : p + 1, :].astype(F32) for p in range(PANELS)]
    mixed = jnp.where((lane < PANEL // 2) == (half == 0), rows[1], FAR)
    order = []
    for column in halves(pivot_columns(pivots_ref))[half]:
        ahead = (rows[2 * half] < column).astype(F32) + (mixed < column).astype(F32)
        order.append(jnp.sum(ahead, axis=1, keepdims=True))
    order = jnp.concatenate(order, axis=0)
    held = lax.broadcasted_iota(jnp.int32, (HALF, HALF), 1).astype(F32)
    return (order == held).astype(BF)


def count_halves(tests):
    return sum(jnp.sum(test.astype(F32), axis=0, keepdims=True) for test in tests)


def pack_kernel(
    turn_ref,
    pivots_hbm,
    points_hbm,
    prior_hbm,
    send_hbm,
    pick_ref,
    turns_ref,
    pivots_ref,
    points_ref,
    prior_ref,
    send_ref,
    sems,
    out_sems,
):
    loads = [
        pltpu.make_async_copy(source, target, sems.at[i])
        for i, (source, target) in enumerate(
            ((pivots_hbm, pivots_ref), (points_hbm, points_ref), (prior_hbm, prior_ref))
        )
    ]
    for load in loads:
        load.start()
    rows = points_ref.shape[0]
    devices = send_ref.shape[0]
    index = lax.axis_index("rows")
    turn = turn_ref[0].astype(F32)
    base = (index * rows).astype(F32)
    loads[0].wait()
    ids = base + lax.broadcasted_iota(jnp.int32, (1, rows), 1).astype(F32)
    homes = devices // 2
    target = lax.broadcasted_iota(jnp.int32, (devices, rows), 0).astype(F32)
    edges = rows * lax.broadcasted_iota(jnp.int32, (1, devices), 1).astype(F32)
    slot = lax.broadcasted_iota(jnp.int32, (8, devices), 0)
    core = lax.rem(index, 2)
    wanted = (index // 2).astype(F32) + homes * slot.astype(F32)
    select, pick, longest = None, None, None
    for half, columns in enumerate(halves(pivot_columns(pivots_ref))):
        place = count_halves([column < ids for column in columns])
        found = count_halves([column == ids for column in columns])
        step = place - place[:, 0:1] - homes * turn
        home = 2.0 * (place - homes * jnp.floor(place * (1.0 / homes))) + half
        home = jnp.where((found > 0.5) & (step >= 0.0) & (step < homes), home, -1.0)
        start = count_halves([column < edges for column in columns])
        stop = count_halves([column < edges + rows for column in columns])
        step = wanted - start - homes * turn
        mine = (wanted >= start) & (wanted < stop) & (step >= 0.0) & (step < homes)
        mine = mine & (slot < HALF // homes) & (core == half)
        hit = target == home
        run = jnp.max(stop - start)
        select = hit if half == 0 else select | hit
        pick = mine if half == 0 else pick | mine
        longest = run if half == 0 else jnp.maximum(longest, run)
    select = select.astype(BF)
    pick_ref[...] = pick.astype(F32)
    turns_ref[0] = jnp.where(longest > 2 * homes, 3, jnp.where(longest > homes, 2, 1))
    at = 0
    stores = []
    for load, ref in ((loads[1], points_ref), (loads[2], prior_ref)):
        load.wait()
        high, mid, low = split3(ref[...])
        got = dot_bf(select, high, NN) + dot_bf(select, mid, NN) + dot_bf(select, low, NN)
        span = slice(at, at + got.shape[1])
        send_ref[:, 0, span] = got
        at += got.shape[1]
        stores.append(
            pltpu.make_async_copy(
                send_ref.at[:, :, span], send_hbm.at[:, :, span], out_sems.at[len(stores)]
            )
        )
        stores[-1].start()
    for store in stores:
        store.wait()


def pick_kernel(pick_ref, came_ref, out_ref, rows_ref):
    rows_ref[...] = came_ref[:, 0, :]
    select = pick_ref[...].astype(BF)
    high, mid, low = split3(rows_ref[...])
    got = dot_bf(select, high, NN) + dot_bf(select, mid, NN) + dot_bf(select, low, NN)
    for row in range(out_ref.shape[2] // F):
        out_ref[0, :, row * F : (row + 1) * F] = got[row : row + 1, :]


def spread_lane(block, lane):
    return jnp.broadcast_to(block[:, lane : lane + 1], (STRIP, PANEL))


def spread_row(block, row):
    return jnp.broadcast_to(block[row : row + 1, :], (STRIP, PANEL))


def factor(w_ref, z_ref, inv_ref):
    size = PANEL
    strips = size // STRIP
    iota = lax.broadcasted_iota(jnp.int32, (STRIP, size), 0)
    z_ref[...] = jnp.zeros_like(z_ref)
    left, right, ready = {}, {}, {}
    for strip in range(strips):
        first = STRIP * strip
        after = first + STRIP
        groups = range(min(LOOK + 1, strips - strip))
        for group in groups:
            if strip + group not in left:
                rows = slice(first + STRIP * group, after + STRIP * group)
                left[strip + group] = w_ref[rows, 0:size]
                right[strip + group] = w_ref[rows, size : 2 * size]
        column = {}
        for group in groups:
            for j in range(STRIP):
                if group == 0 and strip > 0:
                    column[group, j] = ready[j]
                else:
                    column[group, j] = spread_lane(left[strip + group], first + j)
        ready = {}
        if strip + 1 < strips:
            ready = {m: spread_lane(left[strip + 1], after + m) for m in range(STRIP)}
        for j in range(STRIP):
            root = lax.rsqrt(spread_row(column[0, j], j))
            inverse = root * root
            row_left = spread_row(left[strip], j)
            row_right = spread_row(right[strip], j)
            inv_ref[first + j : first + j + 1, :] = row_right[0:1] * root[0:1]
            own = {m: spread_row(column[0, m], j) for m in range(j + 1, STRIP)}
            ahead = {m: spread_row(column[1, j], m) for m in ready}
            for group in groups[0:2]:
                weight = column[group, j] * inverse
                if group == 0:
                    weight = jnp.where(iota == j, 1.0 - inverse, weight)
                for m in own:
                    column[group, m] = column[group, m] - weight * own[m]
                if group == 1:
                    for m in ready:
                        ready[m] = ready[m] - weight * ahead[m]
                left[strip + group] = left[strip + group] - weight * row_left
                right[strip + group] = right[strip + group] - weight * row_right
        for j in range(STRIP):
            for group in groups[2:]:
                weight = column[group, j]
                left[strip + group] = left[strip + group] - weight * spread_row(left[strip], j)
                right[strip + group] = right[strip + group] - weight * spread_row(right[strip], j)
        last = first + STRIP * (LOOK + 1)
        if last < size:
            if strip > 0:
                z_ref[first - STRIP : first, :] = jnp.zeros((STRIP, 2 * size), F32)
            z_ref[first:after, 0:size] = left[strip]
            z_ref[first:after, size : 2 * size] = right[strip]
            update = dot_x3(w_ref[last:size, 0:size], z_ref[...], NN)
            w_ref[last:size, :] = w_ref[last:size, :] - update


def row_of(column):
    return jnp.transpose(jnp.broadcast_to(column, (PANEL, PANEL)))[0:1, :]


def prepare_kernel(
    pivots_ref,
    scale_ref,
    points_ref,
    prior_ref,
    active_ref,
    mine_ref,
    prior2_ref,
    sums_ref,
    place_ref,
    mask_ref,
):
    mask_ref[...] = active_ref[...].astype(F32)
    mine = points_ref[...] * scale_ref[...]
    prior = prior_ref[...]
    for ref, value in ((mine_ref, mine), (prior2_ref, prior)):
        ref[0], ref[1] = split2(value)
    for row, value in enumerate((mine, prior)):
        total = jnp.sum(value * value, axis=1, keepdims=True)
        for i in range(value.shape[0] // 128):
            here = slice(i * 128, (i + 1) * 128)
            sums_ref[row : row + 1, here] = row_of(total[here])
    for half in range(2):
        place_ref[half] = place_in_half(pivots_ref, half)


def half_of(half, noise, pivots_ref, scale_ref, place_ref, sums_ref, mine_ref, prior_ref, buf_ref, g_ref):
    homes = buf_ref.shape[0]
    rows = mine_ref.shape[1]
    for turn in range(HALF // homes):
        g_ref[turn * homes : (turn + 1) * homes, :] = buf_ref[:, 0, turn * F : (turn + 1) * F]
    place = place_ref[half]
    near = [dot_bf(place, part, NN) for part in split2(g_ref[:, 0:D] * scale_ref[...])]
    both = near[0] + near[1]
    near = [part.astype(BF) for part in near]
    factor_rows = [dot_bf(place, part, NN).astype(BF) for part in split2(g_ref[:, D:F])]
    square = jnp.sum(both * both, axis=1, keepdims=True)
    inner = three(near, (mine_ref[0], mine_ref[1]))
    residual = jnp.exp(-0.5 * (square + sums_ref[0:1, :] - 2.0 * inner))
    residual = residual - three(factor_rows, (prior_ref[0], prior_ref[1]))
    first, second = halves(pivot_columns(pivots_ref))
    wanted = jnp.where(half == 0, jnp.concatenate(first, 0), jnp.concatenate(second, 0))
    ids = lax.axis_index("rows") * rows + lax.broadcasted_iota(jnp.int32, (1, rows), 1)
    residual = residual + noise * (wanted == ids.astype(F32)).astype(F32)
    return near, factor_rows, square, residual


def half_kernel(
    noise_ref,
    pivots_ref,
    scale_ref,
    place_ref,
    sums_ref,
    mine_ref,
    prior_ref,
    buf_ref,
    near_ref,
    rows_ref,
    square_ref,
    residual_ref,
    g_ref,
):
    half = lax.rem(lax.axis_index("rows"), 2)
    near, factor_rows, square, residual = half_of(
        half,
        noise_ref[0],
        pivots_ref,
        scale_ref,
        place_ref,
        sums_ref,
        mine_ref,
        prior_ref,
        buf_ref,
        g_ref,
    )
    for part in range(2):
        near_ref[part] = near[part]
        rows_ref[part] = factor_rows[part]
    square_ref[...] = square
    residual_ref[...] = residual


def window_kernel(
    noise_ref,
    pivots_ref,
    scale_ref,
    place_ref,
    sums_ref,
    mine_ref,
    prior_ref,
    buf_ref,
    own_near_ref,
    own_rows_ref,
    own_square_ref,
    own_residual_ref,
    mask_ref,
    new_hbm,
    diag_ref,
    near_ref,
    rows_ref,
    square_ref,
    r_ref,
    g_ref,
    k_ref,
    w_ref,
    z_ref,
    inv_ref,
    x_ref,
    out_sems,
):
    rows = mine_ref.shape[1]
    noise = noise_ref[0]
    core = lax.rem(lax.axis_index("rows"), 2)
    here = pl.ds(pl.multiple_of(core * HALF, HALF), HALF)
    there = pl.ds(pl.multiple_of((1 - core) * HALF, HALF), HALF)
    near, factor_rows, square, residual = half_of(
        1 - core,
        noise,
        pivots_ref,
        scale_ref,
        place_ref,
        sums_ref,
        mine_ref,
        prior_ref,
        buf_ref,
        g_ref,
    )
    for part in range(2):
        near_ref[part, here, :] = own_near_ref[part]
        near_ref[part, there, :] = near[part]
        rows_ref[part, here, :] = own_rows_ref[part]
        rows_ref[part, there, :] = factor_rows[part]
    square_ref[here, :] = own_square_ref[...]
    square_ref[there, :] = square
    r_ref[here, :] = own_residual_ref[...]
    r_ref[there, :] = residual
    square_col = square_ref[...]
    square_row = jnp.concatenate(
        [row_of(square_col[i * PANEL : (i + 1) * PANEL]) for i in range(PANELS)], axis=1
    )
    eye = (
        lax.broadcasted_iota(jnp.int32, (PIV, PIV), 0)
        == lax.broadcasted_iota(jnp.int32, (PIV, PIV), 1)
    ).astype(F32)
    for low, high in ((0, 2 * PANEL), (2 * PANEL, PIV)):
        down, over = slice(low, PIV), slice(low, high)
        inner = three(
            (near_ref[0, down, :], near_ref[1, down, :]),
            (near_ref[0, over, :], near_ref[1, over, :]),
        )
        gram = jnp.exp(-0.5 * (square_col[down] + square_row[:, over] - 2.0 * inner))
        k_ref[down, over] = (gram + noise * eye[down, over]) - three(
            (rows_ref[0, down, :], rows_ref[1, down, :]),
            (rows_ref[0, over, :], rows_ref[1, over, :]),
        )
    small_eye = eye[0:PANEL, 0:PANEL]
    total = sums_ref[1:2, :]
    stores = []
    for panel in range(PANELS):
        span = slice(panel * PANEL, (panel + 1) * PANEL)
        w_ref[:, 0:PANEL] = k_ref[span, span]
        w_ref[:, PANEL:] = small_eye
        factor(w_ref, z_ref, inv_ref)
        inverse = split2(inv_ref[...])
        if panel + 1 < PANELS:
            rest = slice((panel + 1) * PANEL, PIV)
            below = split2(three(split2(k_ref[rest, span]), inverse))
            k_ref[rest, rest] = k_ref[rest, rest] - three(below, below)
        fresh = three(inverse, split2(r_ref[span, :]), NN)
        fresh = fresh * mask_ref[panel : panel + 1, :]
        total = total + jnp.sum(fresh * fresh, axis=0, keepdims=True)
        x_ref[:, span] = jnp.transpose(fresh)
        store = pltpu.make_async_copy(x_ref.at[:, span], new_hbm.at[:, span], out_sems.at[panel])
        store.start()
        stores.append(store)
        if panel + 1 < PANELS:
            r_ref[rest, :] = r_ref[rest, :] - three(below, split2(fresh), NN)
    diag = (1.0 + noise) - total
    for i in range(rows // 128):
        span = slice(i * 128, (i + 1) * 128)
        diag_ref[span] = diag[0, span]
    for store in stores:
        store.wait()


SMEM = pl.BlockSpec(memory_space=pltpu.SMEM)
VMEM = pl.BlockSpec(memory_space=pltpu.VMEM)
SMALL = pltpu.CompilerParams(vmem_limit_bytes=16 * 1024 * 1024)
ANY = pl.BlockSpec(memory_space=pl.ANY)
HBM = pl.BlockSpec(memory_space=pltpu.HBM)


def local(points, inv_scale, noise, prior, active, pivots):
    rows = points.shape[0]
    devices = lax.axis_size("rows")
    homes = devices // 2
    partner = [(i, i ^ 1) for i in range(devices)]
    groups = [[2 * chip + core for chip in range(homes)] for core in range(2)]
    exchange = functools.partial(
        lax.all_to_all, axis_name="rows", split_axis=0, concat_axis=0, tiled=True
    )
    def routed(turn, pivots, points, prior):
        send, pick, turns, *kept = pl.pallas_call(
            pack_kernel,
            out_shape=(
                jax.ShapeDtypeStruct((devices, 1, F), F32),
                jax.ShapeDtypeStruct((8, devices), F32),
                jax.ShapeDtypeStruct((1,), jnp.int32),
                jax.ShapeDtypeStruct((PANELS, PANEL), jnp.int32),
                jax.ShapeDtypeStruct((rows, D), F32),
                jax.ShapeDtypeStruct((rows, R0), F32),
            ),
            in_specs=[SMEM, HBM, HBM, HBM],
            out_specs=(HBM, VMEM, SMEM, VMEM, VMEM, VMEM),
            scratch_shapes=[
                pltpu.VMEM((devices, 1, F), F32),
                pltpu.SemaphoreType.DMA((3,)),
                pltpu.SemaphoreType.DMA((2,)),
            ],
            name="pack",
            compiler_params=SMALL,
        )(turn, pivots, points, prior)
        owned = pl.pallas_call(
            pick_kernel,
            out_shape=jax.ShapeDtypeStruct((1, 1, PIV // devices * F), F32),
            in_specs=[VMEM, VMEM],
            out_specs=VMEM,
            scratch_shapes=[pltpu.VMEM((devices, F), F32)],
            name="pick",
            compiler_params=SMALL,
        )(pick, exchange(send))
        return owned, turns[0], kept

    owned, turns, (pivots, points, prior) = routed(
        jnp.zeros((1,), jnp.int32),
        pltpu.with_memory_space_constraint(pivots, pltpu.HBM),
        pltpu.with_memory_space_constraint(points, pltpu.HBM),
        pltpu.with_memory_space_constraint(prior, pltpu.HBM),
    )

    scale = inv_scale.reshape(1, D)
    mine2, prior2, sums, place, mask = pl.pallas_call(
        prepare_kernel,
        out_shape=(
            jax.ShapeDtypeStruct((2, rows, D), BF),
            jax.ShapeDtypeStruct((2, rows, R0), BF),
            jax.ShapeDtypeStruct((2, rows), F32),
            jax.ShapeDtypeStruct((2, HALF, HALF), BF),
            jax.ShapeDtypeStruct((PANELS, rows), F32),
        ),
        in_specs=[VMEM] * 5,
        out_specs=(VMEM,) * 5,
        name="prepare",
        compiler_params=SMALL,
    )(pivots, scale, points, prior, active)
    owned, mine2, prior2, sums, place, mask = lax.optimization_barrier(
        (owned, mine2, prior2, sums, place, mask)
    )

    def more(state):
        return state[0] < turns

    def again(state):
        turn, owned = state
        return turn + 1, owned + routed(turn[None], pivots, points, prior)[0]

    owned = lax.while_loop(more, again, (jnp.int32(1), owned))[1]
    mine = exchange(jnp.broadcast_to(owned, (homes, *owned.shape[1:])), axis_index_groups=groups)
    other = lax.ppermute(mine, "rows", partner)
    common = (noise, pivots, scale, place, sums, mine2, prior2)
    own = pl.pallas_call(
        half_kernel,
        out_shape=(
            jax.ShapeDtypeStruct((2, HALF, D), BF),
            jax.ShapeDtypeStruct((2, HALF, R0), BF),
            jax.ShapeDtypeStruct((HALF, 1), F32),
            jax.ShapeDtypeStruct((HALF, rows), F32),
        ),
        in_specs=[SMEM] + [VMEM] * 7,
        out_specs=(VMEM,) * 4,
        scratch_shapes=[pltpu.VMEM((HALF, F), F32)],
        name="half",
        compiler_params=SMALL,
    )(*common, mine)
    return pl.pallas_call(
        window_kernel,
        out_shape=(
            jax.ShapeDtypeStruct((rows, PIV), F32),
            jax.ShapeDtypeStruct((rows,), F32),
        ),
        in_specs=[SMEM] + [VMEM] * 12,
        out_specs=(ANY, VMEM),
        scratch_shapes=[
            pltpu.VMEM((2, PIV, D), BF),
            pltpu.VMEM((2, PIV, R0), BF),
            pltpu.VMEM((PIV, 1), F32),
            pltpu.VMEM((PIV, rows), F32),
            pltpu.VMEM((HALF, F), F32),
            pltpu.VMEM((PIV, PIV), F32),
            pltpu.VMEM((PANEL, 2 * PANEL), F32),
            pltpu.VMEM((PANEL, 2 * PANEL), F32),
            pltpu.VMEM((PANEL, PANEL), F32),
            pltpu.VMEM((rows, PIV), F32),
            pltpu.SemaphoreType.DMA((PANELS,)),
        ],
        name="window",
        compiler_params=SMALL,
    )(*common, other, *own, mask)


def solution(mesh):
    return jax.shard_map(
        local,
        mesh=mesh,
        in_specs=(P("rows", None), P(), P(), P("rows", None), P(None, "rows"), P()),
        out_specs=(P("rows", None), P("rows")),
        check_vma=False,
    )
```

```python
import functools

import jax
import jax.numpy as jnp
from jax import lax
from jax.experimental import pallas as pl
from jax.experimental.pallas import tpu as pltpu
from jax.sharding import PartitionSpec as P

D = 256
R0 = 512
F = D + R0
PANEL = 128
PANELS = 3
PIV = PANEL * PANELS
FAR = 1e9
HALF = PIV // 2
STRIP = 8
LOOK = 2
BF = jnp.bfloat16
F32 = jnp.float32
NT = (((1,), (1,)), ((), ()))
NN = (((1,), (0,)), ((), ()))


def split2(a):
    high = a.astype(BF)
    return high, (a - high.astype(F32)).astype(BF)


def split3(a):
    high = a.astype(BF)
    rest = a - high.astype(F32)
    mid = rest.astype(BF)
    return high, mid, (rest - mid.astype(F32)).astype(BF)


def dot_bf(a, b, dims=NT):
    return lax.dot_general(a, b, dims, preferred_element_type=F32)


def dot_x3(a, b, dims=NT):
    return three(split2(a), split2(b), dims)


def three(a, b, dims=NT):
    return dot_bf(a[0], b[0], dims) + (dot_bf(a[0], b[1], dims) + dot_bf(a[1], b[0], dims))


def column_of(row):
    return jnp.transpose(jnp.broadcast_to(row, (8, 128)))[:, 0:1]


def pivot_columns(pivots_ref):
    return [column_of(pivots_ref[p : p + 1, :].astype(F32)) for p in range(PANELS)]


def halves(parts):
    cut = PANEL // 2
    return (
        [parts[0], parts[1][0:cut]],
        [parts[1][cut:PANEL], parts[2]],
    )


def place_in_half(pivots_ref, half):
    lane = lax.broadcasted_iota(jnp.int32, (1, PANEL), 1)
    rows = [pivots_ref[p : p + 1, :].astype(F32) for p in range(PANELS)]
    mixed = jnp.where((lane < PANEL // 2) == (half == 0), rows[1], FAR)
    order = []
    for column in halves(pivot_columns(pivots_ref))[half]:
        ahead = (rows[2 * half] < column).astype(F32) + (mixed < column).astype(F32)
        order.append(jnp.sum(ahead, axis=1, keepdims=True))
    order = jnp.concatenate(order, axis=0)
    held = lax.broadcasted_iota(jnp.int32, (HALF, HALF), 1).astype(F32)
    return (order == held).astype(BF)


def count_halves(tests):
    return sum(jnp.sum(test.astype(F32), axis=0, keepdims=True) for test in tests)


def pack_kernel(
    turn_ref,
    pivots_hbm,
    points_hbm,
    prior_hbm,
    send_hbm,
    pick_ref,
    turns_ref,
    pivots_ref,
    points_ref,
    prior_ref,
    send_ref,
    sems,
    out_sems,
):
    loads = [
        pltpu.make_async_copy(source, target, sems.at[i])
        for i, (source, target) in enumerate(
            ((pivots_hbm, pivots_ref), (points_hbm, points_ref), (prior_hbm, prior_ref))
        )
    ]
    for load in loads:
        load.start()
    rows = points_ref.shape[0]
    devices = send_ref.shape[0]
    index = lax.axis_index("rows")
    turn = turn_ref[0].astype(F32)
    base = (index * rows).astype(F32)
    loads[0].wait()
    ids = base + lax.broadcasted_iota(jnp.int32, (1, rows), 1).astype(F32)
    homes = devices // 2
    target = lax.broadcasted_iota(jnp.int32, (devices, rows), 0).astype(F32)
    edges = rows * lax.broadcasted_iota(jnp.int32, (1, devices), 1).astype(F32)
    slot = lax.broadcasted_iota(jnp.int32, (8, devices), 0)
    core = lax.rem(index, 2)
    wanted = (index // 2).astype(F32) + homes * slot.astype(F32)
    select, pick, longest = None, None, None
    for half, columns in enumerate(halves(pivot_columns(pivots_ref))):
        place = count_halves([column < ids for column in columns])
        found = count_halves([column == ids for column in columns])
        step = place - place[:, 0:1] - homes * turn
        home = 2.0 * (place - homes * jnp.floor(place * (1.0 / homes))) + half
        home = jnp.where((found > 0.5) & (step >= 0.0) & (step < homes), home, -1.0)
        hit = target == home
        select = hit if half == 0 else select | hit
    select = select.astype(BF)
    at = 0
    stores = []
    for load, ref in ((loads[1], points_ref), (loads[2], prior_ref)):
        load.wait()
        high, mid, low = split3(ref[...])
        got = dot_bf(select, high, NN) + dot_bf(select, mid, NN) + dot_bf(select, low, NN)
        span = slice(at, at + got.shape[1])
        send_ref[:, 0, span] = got
        at += got.shape[1]
        stores.append(
            pltpu.make_async_copy(
                send_ref.at[:, :, span], send_hbm.at[:, :, span], out_sems.at[len(stores)]
            )
        )
        stores[-1].start()
    for half, columns in enumerate(halves(pivot_columns(pivots_ref))):
        start = count_halves([column < edges for column in columns])
        stop = count_halves([column < edges + rows for column in columns])
        step = wanted - start - homes * turn
        mine = (wanted >= start) & (wanted < stop) & (step >= 0.0) & (step < homes)
        mine = mine & (slot < HALF // homes) & (core == half)
        run = jnp.max(stop - start)
        pick = mine if half == 0 else pick | mine
        longest = run if half == 0 else jnp.maximum(longest, run)
    pick_ref[...] = pick.astype(F32)
    turns_ref[0] = jnp.where(longest > 2 * homes, 3, jnp.where(longest > homes, 2, 1))
    for store in stores:
        store.wait()


def pick_kernel(pick_ref, came_ref, out_ref, rows_ref):
    rows_ref[...] = came_ref[:, 0, :]
    select = pick_ref[...].astype(BF)
    high, mid, low = split3(rows_ref[...])
    got = dot_bf(select, high, NN) + dot_bf(select, mid, NN) + dot_bf(select, low, NN)
    for row in range(out_ref.shape[2] // F):
        out_ref[0, :, row * F : (row + 1) * F] = got[row : row + 1, :]


def spread_lane(block, lane):
    return jnp.broadcast_to(block[:, lane : lane + 1], (STRIP, PANEL))


def spread_row(block, row):
    return jnp.broadcast_to(block[row : row + 1, :], (STRIP, PANEL))


def factor(w_ref, z_ref, inv_ref):
    size = PANEL
    strips = size // STRIP
    iota = lax.broadcasted_iota(jnp.int32, (STRIP, size), 0)
    z_ref[...] = jnp.zeros_like(z_ref)
    left, right, ready = {}, {}, {}
    for strip in range(strips):
        first = STRIP * strip
        after = first + STRIP
        groups = range(min(LOOK + 1, strips - strip))
        for group in groups:
            if strip + group not in left:
                rows = slice(first + STRIP * group, after + STRIP * group)
                left[strip + group] = w_ref[rows, 0:size]
                right[strip + group] = w_ref[rows, size : 2 * size]
        column = {}
        for group in groups:
            for j in range(STRIP):
                if group == 0 and strip > 0:
                    column[group, j] = ready[j]
                else:
                    column[group, j] = spread_lane(left[strip + group], first + j)
        ready = {}
        if strip + 1 < strips:
            ready = {m: spread_lane(left[strip + 1], after + m) for m in range(STRIP)}
        for j in range(STRIP):
            root = lax.rsqrt(spread_row(column[0, j], j))
            inverse = root * root
            row_left = spread_row(left[strip], j)
            row_right = spread_row(right[strip], j)
            inv_ref[first + j : first + j + 1, :] = row_right[0:1] * root[0:1]
            own = {m: spread_row(column[0, m], j) for m in range(j + 1, STRIP)}
            ahead = {m: spread_row(column[1, j], m) for m in ready}
            for group in groups[0:2]:
                weight = column[group, j] * inverse
                if group == 0:
                    weight = jnp.where(iota == j, 1.0 - inverse, weight)
                for m in own:
                    column[group, m] = column[group, m] - weight * own[m]
                if group == 1:
                    for m in ready:
                        ready[m] = ready[m] - weight * ahead[m]
                left[strip + group] = left[strip + group] - weight * row_left
                right[strip + group] = right[strip + group] - weight * row_right
        for j in range(STRIP):
            for group in groups[2:]:
                weight = column[group, j]
                left[strip + group] = left[strip + group] - weight * spread_row(left[strip], j)
                right[strip + group] = right[strip + group] - weight * spread_row(right[strip], j)
        last = first + STRIP * (LOOK + 1)
        if last < size:
            if strip > 0:
                z_ref[first - STRIP : first, :] = jnp.zeros((STRIP, 2 * size), F32)
            z_ref[first:after, 0:size] = left[strip]
            z_ref[first:after, size : 2 * size] = right[strip]
            update = dot_x3(w_ref[last:size, 0:size], z_ref[...], NN)
            w_ref[last:size, :] = w_ref[last:size, :] - update


def row_of(column):
    return jnp.transpose(jnp.broadcast_to(column, (PANEL, PANEL)))[0:1, :]


def prepare_kernel(
    pivots_ref,
    scale_ref,
    points_ref,
    prior_ref,
    active_ref,
    mine_ref,
    prior2_ref,
    sums_ref,
    place_ref,
    mask_ref,
):
    mask_ref[...] = active_ref[...].astype(F32)
    mine = points_ref[...] * scale_ref[...]
    prior = prior_ref[...]
    for ref, value in ((mine_ref, mine), (prior2_ref, prior)):
        ref[0], ref[1] = split2(value)
    for row, value in enumerate((mine, prior)):
        total = jnp.sum(value * value, axis=1, keepdims=True)
        for i in range(value.shape[0] // 128):
            here = slice(i * 128, (i + 1) * 128)
            sums_ref[row : row + 1, here] = row_of(total[here])
    for half in range(2):
        place_ref[half] = place_in_half(pivots_ref, half)


def half_of(half, noise, pivots_ref, scale_ref, place_ref, sums_ref, mine_ref, prior_ref, buf_ref, g_ref):
    homes = buf_ref.shape[0]
    rows = mine_ref.shape[1]
    for turn in range(HALF // homes):
        g_ref[turn * homes : (turn + 1) * homes, :] = buf_ref[:, 0, turn * F : (turn + 1) * F]
    place = place_ref[half]
    near = [dot_bf(place, part, NN) for part in split2(g_ref[:, 0:D] * scale_ref[...])]
    both = near[0] + near[1]
    near = [part.astype(BF) for part in near]
    factor_rows = [dot_bf(place, part, NN).astype(BF) for part in split2(g_ref[:, D:F])]
    square = jnp.sum(both * both, axis=1, keepdims=True)
    inner = three(near, (mine_ref[0], mine_ref[1]))
    residual = jnp.exp(-0.5 * (square + sums_ref[0:1, :] - 2.0 * inner))
    residual = residual - three(factor_rows, (prior_ref[0], prior_ref[1]))
    first, second = halves(pivot_columns(pivots_ref))
    wanted = jnp.where(half == 0, jnp.concatenate(first, 0), jnp.concatenate(second, 0))
    ids = lax.axis_index("rows") * rows + lax.broadcasted_iota(jnp.int32, (1, rows), 1)
    residual = residual + noise * (wanted == ids.astype(F32)).astype(F32)
    return near, factor_rows, square, residual


def half_kernel(
    noise_ref,
    pivots_ref,
    scale_ref,
    place_ref,
    sums_ref,
    mine_ref,
    prior_ref,
    buf_ref,
    near_ref,
    rows_ref,
    square_ref,
    residual_ref,
    g_ref,
):
    half = lax.rem(lax.axis_index("rows"), 2)
    near, factor_rows, square, residual = half_of(
        half,
        noise_ref[0],
        pivots_ref,
        scale_ref,
        place_ref,
        sums_ref,
        mine_ref,
        prior_ref,
        buf_ref,
        g_ref,
    )
    for part in range(2):
        near_ref[part] = near[part]
        rows_ref[part] = factor_rows[part]
    square_ref[...] = square
    residual_ref[...] = residual


def window_kernel(
    noise_ref,
    pivots_ref,
    scale_ref,
    place_ref,
    sums_ref,
    mine_ref,
    prior_ref,
    buf_ref,
    own_near_ref,
    own_rows_ref,
    own_square_ref,
    own_residual_ref,
    mask_ref,
    new_hbm,
    diag_ref,
    near_ref,
    rows_ref,
    square_ref,
    r_ref,
    g_ref,
    k_ref,
    w_ref,
    z_ref,
    inv_ref,
    x_ref,
    out_sems,
):
    rows = mine_ref.shape[1]
    noise = noise_ref[0]
    core = lax.rem(lax.axis_index("rows"), 2)
    here = pl.ds(pl.multiple_of(core * HALF, HALF), HALF)
    there = pl.ds(pl.multiple_of((1 - core) * HALF, HALF), HALF)
    near, factor_rows, square, residual = half_of(
        1 - core,
        noise,
        pivots_ref,
        scale_ref,
        place_ref,
        sums_ref,
        mine_ref,
        prior_ref,
        buf_ref,
        g_ref,
    )
    for part in range(2):
        near_ref[part, here, :] = own_near_ref[part]
        near_ref[part, there, :] = near[part]
        rows_ref[part, here, :] = own_rows_ref[part]
        rows_ref[part, there, :] = factor_rows[part]
    square_ref[here, :] = own_square_ref[...]
    square_ref[there, :] = square
    r_ref[here, :] = own_residual_ref[...]
    r_ref[there, :] = residual
    square_col = square_ref[...]
    square_row = jnp.concatenate(
        [row_of(square_col[i * PANEL : (i + 1) * PANEL]) for i in range(PANELS)], axis=1
    )
    eye = (
        lax.broadcasted_iota(jnp.int32, (PIV, PIV), 0)
        == lax.broadcasted_iota(jnp.int32, (PIV, PIV), 1)
    ).astype(F32)
    for low, high in ((0, 2 * PANEL), (2 * PANEL, PIV)):
        down, over = slice(low, PIV), slice(low, high)
        inner = three(
            (near_ref[0, down, :], near_ref[1, down, :]),
            (near_ref[0, over, :], near_ref[1, over, :]),
        )
        gram = jnp.exp(-0.5 * (square_col[down] + square_row[:, over] - 2.0 * inner))
        k_ref[down, over] = (gram + noise * eye[down, over]) - three(
            (rows_ref[0, down, :], rows_ref[1, down, :]),
            (rows_ref[0, over, :], rows_ref[1, over, :]),
        )
    small_eye = eye[0:PANEL, 0:PANEL]
    total = sums_ref[1:2, :]
    stores = []
    for panel in range(PANELS):
        span = slice(panel * PANEL, (panel + 1) * PANEL)
        w_ref[:, 0:PANEL] = k_ref[span, span]
        w_ref[:, PANEL:] = small_eye
        factor(w_ref, z_ref, inv_ref)
        inverse = split2(inv_ref[...])
        if panel + 1 < PANELS:
            rest = slice((panel + 1) * PANEL, PIV)
            below = split2(three(split2(k_ref[rest, span]), inverse))
            k_ref[rest, rest] = k_ref[rest, rest] - three(below, below)
        fresh = three(inverse, split2(r_ref[span, :]), NN)
        fresh = fresh * mask_ref[panel : panel + 1, :]
        total = total + jnp.sum(fresh * fresh, axis=0, keepdims=True)
        x_ref[:, span] = jnp.transpose(fresh)
        store = pltpu.make_async_copy(x_ref.at[:, span], new_hbm.at[:, span], out_sems.at[panel])
        store.start()
        stores.append(store)
        if panel + 1 < PANELS:
            r_ref[rest, :] = r_ref[rest, :] - three(below, split2(fresh), NN)
    diag = (1.0 + noise) - total
    for i in range(rows // 128):
        span = slice(i * 128, (i + 1) * 128)
        diag_ref[span] = diag[0, span]
    for store in stores:
        store.wait()


SMEM = pl.BlockSpec(memory_space=pltpu.SMEM)
VMEM = pl.BlockSpec(memory_space=pltpu.VMEM)
SMALL = pltpu.CompilerParams(vmem_limit_bytes=16 * 1024 * 1024)
ANY = pl.BlockSpec(memory_space=pl.ANY)
HBM = pl.BlockSpec(memory_space=pltpu.HBM)


def local(points, inv_scale, noise, prior, active, pivots):
    rows = points.shape[0]
    devices = lax.axis_size("rows")
    homes = devices // 2
    partner = [(i, i ^ 1) for i in range(devices)]
    groups = [[2 * chip + core for chip in range(homes)] for core in range(2)]
    exchange = functools.partial(
        lax.all_to_all, axis_name="rows", split_axis=0, concat_axis=0, tiled=True
    )
    def routed(turn, pivots, points, prior):
        send, pick, turns, *kept = pl.pallas_call(
            pack_kernel,
            out_shape=(
                jax.ShapeDtypeStruct((devices, 1, F), F32),
                jax.ShapeDtypeStruct((8, devices), F32),
                jax.ShapeDtypeStruct((1,), jnp.int32),
                jax.ShapeDtypeStruct((PANELS, PANEL), jnp.int32),
                jax.ShapeDtypeStruct((rows, D), F32),
                jax.ShapeDtypeStruct((rows, R0), F32),
            ),
            in_specs=[SMEM, HBM, HBM, HBM],
            out_specs=(HBM, VMEM, SMEM, VMEM, VMEM, VMEM),
            scratch_shapes=[
                pltpu.VMEM((devices, 1, F), F32),
                pltpu.SemaphoreType.DMA((3,)),
                pltpu.SemaphoreType.DMA((2,)),
            ],
            name="pack",
            compiler_params=SMALL,
        )(turn, pivots, points, prior)
        owned = pl.pallas_call(
            pick_kernel,
            out_shape=jax.ShapeDtypeStruct((1, 1, PIV // devices * F), F32),
            in_specs=[VMEM, VMEM],
            out_specs=VMEM,
            scratch_shapes=[pltpu.VMEM((devices, F), F32)],
            name="pick",
            compiler_params=SMALL,
        )(pick, exchange(send))
        return owned, turns[0], kept

    owned, turns, (pivots, points, prior) = routed(
        jnp.zeros((1,), jnp.int32),
        pltpu.with_memory_space_constraint(pivots, pltpu.HBM),
        pltpu.with_memory_space_constraint(points, pltpu.HBM),
        pltpu.with_memory_space_constraint(prior, pltpu.HBM),
    )

    scale = inv_scale.reshape(1, D)
    mine2, prior2, sums, place, mask = pl.pallas_call(
        prepare_kernel,
        out_shape=(
            jax.ShapeDtypeStruct((2, rows, D), BF),
            jax.ShapeDtypeStruct((2, rows, R0), BF),
            jax.ShapeDtypeStruct((2, rows), F32),
            jax.ShapeDtypeStruct((2, HALF, HALF), BF),
            jax.ShapeDtypeStruct((PANELS, rows), F32),
        ),
        in_specs=[VMEM] * 5,
        out_specs=(VMEM,) * 5,
        name="prepare",
        compiler_params=SMALL,
    )(pivots, scale, points, prior, active)
    owned, mine2, prior2, sums, place, mask = lax.optimization_barrier(
        (owned, mine2, prior2, sums, place, mask)
    )

    def more(state):
        return state[0] < turns

    def again(state):
        turn, owned = state
        return turn + 1, owned + routed(turn[None], pivots, points, prior)[0]

    owned = lax.while_loop(more, again, (jnp.int32(1), owned))[1]
    mine = exchange(jnp.broadcast_to(owned, (homes, *owned.shape[1:])), axis_index_groups=groups)
    other = lax.ppermute(mine, "rows", partner)
    common = (noise, pivots, scale, place, sums, mine2, prior2)
    own = pl.pallas_call(
        half_kernel,
        out_shape=(
            jax.ShapeDtypeStruct((2, HALF, D), BF),
            jax.ShapeDtypeStruct((2, HALF, R0), BF),
            jax.ShapeDtypeStruct((HALF, 1), F32),
            jax.ShapeDtypeStruct((HALF, rows), F32),
        ),
        in_specs=[SMEM] + [VMEM] * 7,
        out_specs=(VMEM,) * 4,
        scratch_shapes=[pltpu.VMEM((HALF, F), F32)],
        name="half",
        compiler_params=SMALL,
    )(*common, mine)
    return pl.pallas_call(
        window_kernel,
        out_shape=(
            jax.ShapeDtypeStruct((rows, PIV), F32),
            jax.ShapeDtypeStruct((rows,), F32),
        ),
        in_specs=[SMEM] + [VMEM] * 12,
        out_specs=(ANY, VMEM),
        scratch_shapes=[
            pltpu.VMEM((2, PIV, D), BF),
            pltpu.VMEM((2, PIV, R0), BF),
            pltpu.VMEM((PIV, 1), F32),
            pltpu.VMEM((PIV, rows), F32),
            pltpu.VMEM((HALF, F), F32),
            pltpu.VMEM((PIV, PIV), F32),
            pltpu.VMEM((PANEL, 2 * PANEL), F32),
            pltpu.VMEM((PANEL, 2 * PANEL), F32),
            pltpu.VMEM((PANEL, PANEL), F32),
            pltpu.VMEM((rows, PIV), F32),
            pltpu.SemaphoreType.DMA((PANELS,)),
        ],
        name="window",
        compiler_params=SMALL,
    )(*common, other, *own, mask)


def solution(mesh):
    return jax.shard_map(
        local,
        mesh=mesh,
        in_specs=(P("rows", None), P(), P(), P("rows", None), P(None, "rows"), P()),
        out_specs=(P("rows", None), P("rows")),
        check_vma=False,
    )
```
